512 devices in a mesh: dp: 16 (over y, core), table: 32 (over x, z).
Axes of the slice: x: 4, y: 8, z: 8, core: 2. Of those that a mesh axis runs over, the one named last changes fastest.
Arguments:
- bag_slots: int32 [262144, 32], P(('dp', 'table')), may hold values from -1 to 3071
- labels: float32 [262144], P(('dp', 'table')), may hold values from 0 to 1
- cold_ids: int32 [512, 32, 32], P(('dp', 'table')), may hold values from 0 to 1023
- cold_count: int32 [512, 32], P(('dp', 'table')), may hold values from 1 to 32, 512 in all within a row
- table: float32 [32768, 256], P('table'), may hold values from -1.8 to 1.8
- adagrad_sum: float32 [32768], P('table'), may hold values from 0.1 to 10
- hot_ids: int32 [2048], P('table'), may hold values from 0 to 1023
- w_in: bfloat16 [256, 4096], replicated, may hold values from -0.375 to 0.375
- w_out: bfloat16 [4096], replicated, may hold values from -0.09375 to 0.09375
Outputs:
- new_table: float32 [32768, 256], P('table')
- new_sum: float32 [32768], P('table')
The draws below stay inside these ranges and needn't reach their ends.
Inputs may be any that keep to these rules, and one draw needn't show every extreme that they name: `bag_slots`: -1 marks an empty bag entry. `cold_count`: each reader's counts sum to 512.
All inputs are finite; a program needn't handle non-finite values.
Results may differ from the reference program's by a relative error of at most 0.0045.
The reference program's roundings to bfloat16 on the way count: a program that leaves them out, or rounds other values in their place, can miss the bound.
Values may be sent and summed in bfloat16 or wider, within the bound.
A program may use at most 64 MiB of HBM per device.

```python
import math
import jax
import jax.numpy as jnp
import numpy as np
from jax import lax

E = 256
H = 4096
B_DEV = 512
BAG = 32
ROWS_DEV = 1024
HOT_DEV = 64
C = 32
ROWS = 32768
TOKENS = 262144
VOCAB = 3072
N_DP = 16
N_TABLE = 32


def touch_ends(values, stream_key, low, top_value):
    index_at = [jax.random.randint(jax.random.fold_in(stream_key, axis), (), 0, length) for axis, length in enumerate(values.shape)]
    widest = values.shape.index(max(values.shape))
    next_to = index_at[:widest] + [(index_at[widest] + 1) % values.shape[widest]] + index_at[widest + 1:]
    return values.at[tuple(index_at)].set(low).at[tuple(next_to)].set(top_value)


def levels(own_key, shape, shards, least, top_value):
    gain = 1.0
    for position, parts in shards:
        heights = jax.random.uniform(jax.random.fold_in(jax.random.fold_in(own_key, 6), position), (parts,), jnp.float32, least / len(shards), top_value / len(shards))
        gain = gain * jnp.repeat(jnp.exp(heights), shape[position] // parts).reshape((-1,) + (1,) * (len(shape) - 1 - position))
    return gain


def split_up(count, total, reach, slope):
    loads = [(1 << 20) // math.isqrt(grade ** slope) + 1 for grade in range(2, count + 1)]
    surplus, given = total - reach - (count - 1), [1] * (count - 1)
    while surplus > 0:
        free = [i for i in range(count - 1) if given[i] < reach]
        whole, budget = sum([loads[i] for i in free]), surplus
        for i in free:
            extra = min(reach - given[i], max(1, budget * loads[i] // whole), surplus)
            given[i] = given[i] + extra
            surplus = surplus - extra
    return np.array([reach] + given)


def uneven(rng, number_of, total, limit, skew):
    if number_of == 2:
        one = jax.random.randint(rng, (), max(1, total - limit), min(limit, total - 1) + 1)
        return jnp.stack([one, total - one])
    lengths = jnp.asarray(split_up(number_of, total, limit, skew), jnp.int32)
    couples = (number_of - 1) // 2
    source_of, receiver = lengths[1:1 + 2 * couples:2], lengths[2:2 + 2 * couples:2]
    margin = jnp.minimum(source_of - 1, limit - receiver)
    passed = jax.random.randint(jax.random.fold_in(rng, 1), (couples,), 0, 1 << 20) % (margin + 1)
    lengths = lengths.at[1:1 + 2 * couples:2].set(source_of - passed).at[2:2 + 2 * couples:2].set(receiver + passed)
    return lengths[jax.random.permutation(jax.random.fold_in(rng, 2), number_of)]


def bell_draw(own_key, extent, spread, limit, cuts=(), kind=jnp.bfloat16):
    entries = jax.random.normal(own_key, extent, jnp.float32) * spread
    if len(cuts) > 0:
        entries = levels(own_key, extent, cuts, -0.22, 0.18) * entries
    return jnp.clip(entries, min=-limit, max=limit).astype(kind)


def setup_inputs(seed: int = 0) -> dict:
    streams_of = jax.random.split(jax.random.key(seed), 10)
    bag_slots = touch_ends(jax.random.randint(streams_of[0], (TOKENS, BAG), -1, VOCAB), jax.random.fold_in(streams_of[0], 1), -1, VOCAB - 1).astype(jnp.int32)
    labels = jnp.clip(1.0 * jax.random.uniform(streams_of[1], (TOKENS,), jnp.float32) ** levels(streams_of[1], (TOKENS,), ((0, 512),), -0.2, 0.2), 0.0, 1.0)
    cold_ids = touch_ends(jax.random.randint(streams_of[2], (N_DP * N_TABLE, N_TABLE, C), 0, ROWS_DEV), jax.random.fold_in(streams_of[2], 1), 0, ROWS_DEV - 1).astype(jnp.int32)
    cold_count = jax.vmap(lambda own: uneven(own, N_TABLE, C * N_TABLE // 2, C, 2))(jax.random.split(streams_of[3], (N_DP * N_TABLE))).reshape((N_DP * N_TABLE, N_TABLE)).astype(jnp.int32)
    table = bell_draw(streams_of[4], (ROWS, E), 0.3, 1.8, ((0, 32),), jnp.float32)
    adagrad_sum = jnp.clip(jnp.exp(math.log(10.0) - 4.6051702 * jax.random.uniform(streams_of[5], (ROWS,), jnp.float32) ** levels(streams_of[5], (ROWS,), ((0, 32),), -0.2, 0.2)), 0.1, 10.0)
    hot_ids = touch_ends(jax.random.randint(streams_of[6], (N_TABLE * HOT_DEV,), 0, ROWS_DEV), jax.random.fold_in(streams_of[6], 1), 0, ROWS_DEV - 1).astype(jnp.int32)
    w_in = bell_draw(streams_of[7], (E, H), E ** -0.5, 0.375)
    w_out = bell_draw(streams_of[8], (H,), H ** -0.5, 0.09375)
    return {"bag_slots": bag_slots, "labels": labels, "cold_ids": cold_ids, "cold_count": cold_count, "table": table, "adagrad_sum": adagrad_sum, "hot_ids": hot_ids, "w_in": w_in, "w_out": w_out}


learning_rate = 0.3

def reference(bag_slots, labels, cold_ids, cold_count, table, adagrad_sum, hot_ids, w_in, w_out):
    readers = N_DP * N_TABLE
    hot_total = N_TABLE * HOT_DEV
    owner_base = jnp.arange(N_TABLE, dtype=jnp.int32) * ROWS_DEV
    hot_global = (jnp.repeat(owner_base, HOT_DEV) + hot_ids).astype(jnp.int32)
    table_bf = table.astype(jnp.bfloat16)
    slot_iota = jnp.arange(C, dtype=jnp.int32)
    w_out_f = w_out.astype(jnp.float32)

    def one_reader(grad, reader):
        slots = lax.dynamic_slice_in_dim(bag_slots, reader * B_DEV, B_DEV, 0)
        targets = lax.dynamic_slice_in_dim(labels, reader * B_DEV, B_DEV, 0)
        cold_global = (owner_base[:, None] + cold_ids[reader]).reshape(-1).astype(jnp.int32)
        cold_live = (slot_iota[None, :] < cold_count[reader][:, None]).reshape(-1)
        vocab_ids = jnp.concatenate([hot_global, cold_global])
        vocab_live = jnp.concatenate([jnp.ones((hot_total,), bool), cold_live])
        safe = jnp.maximum(slots, 0)
        entry_ids = vocab_ids[safe]
        entry_live = (slots >= 0) & vocab_live[safe]
        entry_rows = jnp.where(entry_live[..., None], table_bf[entry_ids].astype(jnp.float32), 0.0)
        pooled = lax.optimization_barrier(jnp.sum(entry_rows, axis=1)).astype(jnp.bfloat16)
        pre_act = jnp.dot(pooled, w_in, preferred_element_type=jnp.float32)
        hidden = jax.nn.relu(pre_act).astype(jnp.bfloat16)
        logit = jnp.dot(hidden, w_out, preferred_element_type=jnp.float32)
        dlogit = jax.nn.sigmoid(logit) - targets
        dhidden = (dlogit[:, None] * w_out_f[None, :] * (pre_act > 0)).astype(jnp.bfloat16)
        dpooled = jnp.dot(dhidden, w_in.T, preferred_element_type=jnp.float32).astype(jnp.bfloat16)
        contrib = jnp.where(entry_live[..., None], dpooled.astype(jnp.float32)[:, None, :], 0.0)
        grad = grad.at[entry_ids.reshape(-1)].add(contrib.reshape(-1, E))
        return (grad, None)
    grad, _ = lax.scan(one_reader, jnp.zeros((ROWS, E), jnp.float32), jnp.arange(readers, dtype=jnp.int32))
    new_sum = adagrad_sum + lax.optimization_barrier(jnp.mean(grad * grad, axis=1))
    new_table = table - learning_rate * grad / jnp.sqrt(new_sum)[:, None]
    return (new_table, new_sum)
```

```python
import functools

import jax
import jax.numpy as jnp
from jax import lax
from jax.experimental import pallas as pl
from jax.experimental.pallas import tpu as pltpu
from jax.sharding import PartitionSpec as P

MESH = pl.DeviceIdType.MESH
learning_rate = 0.3
NX, NZ, NY = 4, 8, 8
bf16, f32, i32 = jnp.bfloat16, jnp.float32, jnp.int32


def remote(src, dst, send_sem, recv_sem, dp, table):
    return pltpu.make_async_remote_copy(
        src_ref=src,
        dst_ref=dst,
        send_sem=send_sem,
        recv_sem=recv_sem,
        device_id=(dp, table),
        device_id_type=MESH,
    )


def peer(k, x, z):
    m = k // NX
    kz = (NZ // 2 + (1 - 2 * (m % 2)) * ((m + 1) // 2)) % NZ
    kx = (k + 1) % NX
    return ((x + kx) % NX) * NZ + (z + kz) % NZ


def place():
    dp, me = lax.axis_index("dp"), lax.axis_index("table")
    y, c = dp // 2, dp % 2
    x, z = me // NZ, me % NZ
    partner = y * 2 + (1 - c)
    return dp, me, y, c, x, z, partner


def fetch_kernel(
    table_ref, hot_ids_ref, ids_ref, hot_ref, fetched_ref, asked_ref,
    tb, oh, served,
    ids_s, ids_r, za_s, za_r, xb_s, xb_r, cc_s, cc_r, f_s, f_r,
):
    n = NX * NZ
    dp, me, y, c, x, z, partner = place()
    barrier = pltpu.get_barrier_semaphore()

    def greet(k, _):
        pl.semaphore_signal(barrier, inc=1, device_id=(dp, peer(k, x, z)), device_id_type=MESH)
        return 0

    lax.fori_loop(0, n - 1, greet, 0)
    pl.semaphore_signal(barrier, inc=1, device_id=(partner, me), device_id_type=MESH)

    rows, width = table_ref.shape
    half = hot_ids_ref.shape[1]
    slots = fetched_ref.shape[1]
    tb[...] = table_ref[...].astype(bf16)
    hot_sel = (hot_ids_ref[c] == lax.broadcasted_iota(i32, (half, rows), 1)).astype(f32).astype(bf16)
    hot_ref[x, z, c] = jnp.dot(hot_sel, tb[...], preferred_element_type=f32).astype(bf16)
    asked_ref[me] = ids_ref[me]
    pl.semaphore_wait(barrier, n)

    def send_ids(k, _):
        p = peer(k, x, z)
        remote(ids_ref.at[p], asked_ref.at[me], ids_s.at[p], ids_r.at[me], dp, p).start()
        return 0

    lax.fori_loop(0, n - 1, send_ids, 0)

    def hot_to_x(zs, xo):
        xt = (x + xo) % NX
        blk = hot_ref.at[x, zs, c]
        remote(blk, blk, xb_s.at[xo, zs], xb_r.at[x, zs], dp, xt * NZ + z).start()

    for zo in range(1, NZ):
        zt = (z + zo) % NZ
        blk = hot_ref.at[x, z, c]
        remote(blk, blk, za_s.at[zo], za_r.at[z], dp, x * NZ + zt).start()
    for xo in range(1, NX):
        hot_to_x(z, xo)

    def forward_x(zo, _):
        zs = (z + zo) % NZ
        blk = hot_ref.at[x, zs, c]
        remote(blk, blk, za_s.at[zo], za_r.at[zs], dp, me).wait_recv()
        for xo in range(1, NX):
            hot_to_x(zs, xo)
        return 0

    lax.fori_loop(1, NZ, forward_x, 0)
    line = hot_ref.at[x, :, c]
    remote(line, line, cc_s.at[x], cc_r.at[x], partner, me).start()

    eye = lax.broadcasted_iota(i32, (slots, 128), 0) == lax.broadcasted_iota(i32, (slots, 128), 1)
    chunk = served.shape[1] // slots

    def serve(ch, _):
        for j in range(chunk):
            k = ch * chunk + j
            p = peer(k, x, z)

            def arrived():
                remote(ids_ref.at[p], asked_ref.at[p], ids_s.at[p], ids_r.at[p], dp, p).wait_recv()

            if j == chunk - 1:
                pl.when(k < n - 1)(arrived)
            else:
                arrived()
            row = asked_ref[p].astype(f32)
            col = jnp.sum(jnp.where(eye, row, 0.0), axis=1, keepdims=True)
            hit = col == lax.broadcasted_iota(i32, (slots, rows), 1).astype(f32)
            oh[pl.ds(j * slots, slots), :] = hit.astype(f32).astype(bf16)
        served[ch] = jnp.dot(oh[...], tb[...], preferred_element_type=f32).astype(bf16)
        for j in range(chunk):
            k = ch * chunk + j
            p = peer(k, x, z)
            block = served.at[ch, pl.ds(j * slots, slots)]

            def send():
                remote(block, fetched_ref.at[me], f_s.at[p], f_r.at[me], dp, p).start()

            def keep():
                fetched_ref[me] = served[ch, pl.ds(j * slots, slots)]

            if j == chunk - 1:
                pl.when(k < n - 1)(send)
                pl.when(k == n - 1)(keep)
            else:
                send()
        return 0

    lax.fori_loop(0, n // chunk, serve, 0)

    def line_to_partner(xo, _):
        xs = (x + xo) % NX

        def landed(zs, _):
            blk = hot_ref.at[xs, zs, c]
            remote(blk, blk, xb_s.at[xo, zs], xb_r.at[xs, zs], dp, me).wait_recv()
            return 0

        lax.fori_loop(0, NZ, landed, 0)
        line = hot_ref.at[xs, :, c]
        remote(line, line, cc_s.at[xs], cc_r.at[xs], partner, me).start()
        return 0

    lax.fori_loop(1, NX, line_to_partner, 0)

    def finish_x(xs, _):
        line = hot_ref.at[xs, :, 1 - c]
        remote(line, line, cc_s.at[xs], cc_r.at[xs], partner, me).wait_recv()
        mine = hot_ref.at[xs, :, c]
        remote(mine, mine, cc_s.at[xs], cc_r.at[xs], partner, me).wait_send()
        return 0

    lax.fori_loop(0, NX, finish_x, 0)

    def finish(k, _):
        p = peer(k, x, z)
        remote(served.at[0, pl.ds(0, slots)], fetched_ref.at[p], f_s.at[p], f_r.at[p], dp, p).wait_recv()
        remote(ids_ref.at[p], asked_ref.at[me], ids_s.at[p], ids_r.at[me], dp, p).wait_send()
        remote(served.at[0, pl.ds(0, slots)], fetched_ref.at[me], f_s.at[p], f_r.at[me], dp, p).wait_send()
        return 0

    lax.fori_loop(0, n - 1, finish, 0)

    def finish_hot(zo, _):
        blk = hot_ref.at[x, z, c]
        zs = (z + zo) % NZ

        @pl.when(zo > 0)
        def _():
            remote(blk, blk, za_s.at[zo], za_r.at[z], dp, me).wait_send()

        for xo in range(1, NX):
            remote(blk, blk, xb_s.at[xo, zs], xb_r.at[x, zs], dp, me).wait_send()
        return 0

    lax.fori_loop(0, NZ, finish_hot, 0)


def fetch(table, hot_ids, ids):
    n = NX * NZ
    rows, width = table.shape
    slots = ids.shape[1]
    half = hot_ids.shape[0] // 2
    chunk = min(8, n)
    ids3 = jnp.pad(ids, ((0, 0), (0, 128 - slots)), constant_values=-1).reshape(n, 1, 128)
    dma = pltpu.SemaphoreType.DMA
    vmem = pl.BlockSpec(memory_space=pltpu.VMEM)
    return pl.pallas_call(
        fetch_kernel,
        name="fetch",
        out_shape=(
            jax.ShapeDtypeStruct((NX, NZ, 2, half, width), bf16),
            jax.ShapeDtypeStruct((n, slots, width), bf16),
            jax.ShapeDtypeStruct((n, 1, 128), i32),
        ),
        in_specs=[vmem] * 3,
        out_specs=(vmem,) * 3,
        scratch_shapes=[
            pltpu.VMEM((rows, width), bf16),
            pltpu.VMEM((chunk * slots, rows), bf16),
            pltpu.VMEM((n // chunk, chunk * slots, width), bf16),
            dma((n,)), dma((n,)),
            dma((NZ,)), dma((NZ,)),
            dma((NX, NZ)), dma((NX, NZ)),
            dma((NX,)), dma((NX,)),
            dma((n,)), dma((n,)),
        ],
        compiler_params=pltpu.CompilerParams(collective_id=0, has_side_effects=True),
    )(table, hot_ids.reshape(2, half, 1), ids3)


def mlp_kernel(
    bag_ref, live_ref, hot_ref, cold_ref, labels_ref, w_in_ref, w_out_ref,
    hot_g_ref, cold_g_ref,
    inc, wm, acc, dpool,
):
    batch, vocab = inc.shape
    hot_cols = hot_ref.shape[0]
    width = hot_ref.shape[1]
    hidden_units = w_in_ref.shape[1]
    tiles = vocab // 128
    hot_tiles = hot_cols // 128
    entries = bag_ref.shape[1]
    bag = entries // 8
    sub = lax.broadcasted_iota(i32, (8, entries), 0)
    own = lax.broadcasted_iota(i32, (8, entries), 1) // bag == sub
    tile_ids = lax.broadcasted_iota(i32, (tiles, 8, entries), 0)
    lane_ids = lax.broadcasted_iota(i32, (128, entries), 0)

    def build(i, _):
        outs = []
        for h in range(2):
            v = bag_ref[pl.ds(2 * i + h, 1), :]
            key = jnp.where(own, v >> 7, -1)
            left = (key[None] == tile_ids).astype(f32).reshape(tiles * 8, entries).astype(bf16)
            right = (lane_ids == (v & 127)).astype(f32).astype(bf16)
            outs.append(
                lax.dot_general(left, right, (((1,), (1,)), ((), ())), preferred_element_type=f32)
            )
        at = pl.ds(pl.multiple_of(16 * i, 16), 16)
        for k in range(tiles):
            t = jnp.concatenate([outs[0][8 * k : 8 * k + 8], outs[1][8 * k : 8 * k + 8]], axis=0)
            if k >= hot_tiles:
                t = t * live_ref[:, pl.ds((k - hot_tiles) * 128, 128)]
            inc[at, pl.ds(k * 128, 128)] = t.astype(bf16)
        return 0

    lax.fori_loop(0, batch // 16, build, 0)

    pooled = (
        jnp.dot(inc[:, pl.ds(0, hot_cols)], hot_ref[...], preferred_element_type=f32)
        + jnp.dot(inc[:, pl.ds(hot_cols, vocab - hot_cols)], cold_ref[...], preferred_element_type=f32)
    ).astype(bf16)
    acc[...] = jnp.zeros_like(acc)
    step = acc.shape[1]

    def forward(j, _):
        at = pl.ds(pl.multiple_of(j * step, step), step)
        pre = jnp.dot(pooled, w_in_ref[:, at], preferred_element_type=f32)
        w = w_out_ref[:, at].astype(f32)
        acc[...] += jnp.maximum(pre, 0.0).astype(bf16).astype(f32) * w
        wm[:, at] = jnp.where(pre > 0, w, 0.0).astype(bf16)
        return 0

    lax.fori_loop(0, hidden_units // step, forward, 0)
    logit = jnp.sum(acc[...], axis=1, keepdims=True)
    dlogit = jax.nn.sigmoid(logit) - labels_ref[...]
    dpool[...] = jnp.zeros_like(dpool)

    def backward(j, _):
        at = pl.ds(pl.multiple_of(j * step, step), step)
        dhidden = (dlogit * wm[:, at].astype(f32)).astype(bf16)
        dpool[...] += lax.dot_general(
            dhidden, w_in_ref[:, at], (((1,), (1,)), ((), ())), preferred_element_type=f32
        )
        return 0

    lax.fori_loop(0, hidden_units // step, backward, 0)
    dpooled = dpool[...].astype(bf16)

    for k in range(vocab // 256):
        g = lax.dot_general(
            inc[:, pl.ds(k * 256, 256)], dpooled, (((0,), (0,)), ((), ())), preferred_element_type=f32
        ).astype(bf16)
        if k * 256 < hot_cols:
            for h in range(2):
                hot_g_ref[h, pl.ds(k * 256, 256), :] = g[:, h * 128 : (h + 1) * 128]
        else:
            cold_g_ref[pl.ds(k * 256 - hot_cols, 256), :] = g


def mlp(bag_slots, live, hot_rows, cold_rows, labels, w_in, w_out):
    batch, bag = bag_slots.shape
    hot_cols, width = hot_rows.shape
    cold_cols = cold_rows.shape[0]
    vmem = pl.BlockSpec(memory_space=pltpu.VMEM)
    return pl.pallas_call(
        mlp_kernel,
        name="mlp",
        out_shape=(
            jax.ShapeDtypeStruct((2, hot_cols, 128), bf16),
            jax.ShapeDtypeStruct((cold_cols, width), bf16),
        ),
        in_specs=[vmem] * 7,
        out_specs=(vmem,) * 2,
        scratch_shapes=[
            pltpu.VMEM((batch, hot_cols + cold_cols), bf16),
            pltpu.VMEM((batch, w_in.shape[1]), bf16),
            pltpu.VMEM((batch, 256), f32),
            pltpu.VMEM((batch, width), f32),
        ],
        compiler_params=pltpu.CompilerParams(vmem_limit_bytes=48 << 20),
    )(
        bag_slots.reshape(batch // 8, 8 * bag),
        live,
        hot_rows,
        cold_rows,
        labels.reshape(batch, 1),
        w_in,
        w_out.reshape(1, -1),
    )


def reduce_kernel(
    hot_g, cold_g, asked_ref, hot_pad_ref, total_ref,
    hcore, hsum, hy, hz, ht, ret, oht, gl, gcore, gsum, gy, hfin,
    hc_s, hc_r, hy_s, hy_r, ht_s, ht_r, c_s, c_r, gc_s, gc_r, gy_s, gy_r, ag_s, ag_r, ac_s, ac_r,
):
    n = NX * NZ
    dp, me, y, c, x, z, partner = place()
    barrier = pltpu.get_barrier_semaphore()

    def dp_of(yy):
        return yy * 2 + c

    def greet(k, _):
        pl.semaphore_signal(barrier, inc=1, device_id=(dp, peer(k, x, z)), device_id_type=MESH)
        return 0

    lax.fori_loop(0, n - 1, greet, 0)

    def greet_y(k, _):
        pl.semaphore_signal(barrier, inc=1, device_id=(dp_of((y + k) % NY), me), device_id_type=MESH)
        return 0

    lax.fori_loop(1, NY, greet_y, 0)
    pl.semaphore_signal(barrier, inc=1, device_id=(partner, me), device_id_type=MESH)
    pl.semaphore_wait(barrier, n - 1 + NY)

    def core_send(k, _):
        yt = (y + k) % NY
        remote(hot_g.at[1 - c, :, yt], hcore.at[yt], hc_s.at[yt], hc_r.at[yt], partner, me).start()
        return 0

    lax.fori_loop(0, NY, core_send, 0)

    def cold_send(k, _):
        p = peer(k, x, z)
        remote(cold_g.at[p], ret.at[me], c_s.at[p], c_r.at[me], dp, p).start()
        return 0

    lax.fori_loop(0, n - 1, cold_send, 0)

    def y_send(k, _):
        yt = (y + k) % NY
        remote(hot_g.at[1 - c, :, yt], hcore.at[yt], hc_s.at[yt], hc_r.at[yt], partner, me).wait_recv()
        hsum[yt] = (hot_g[c, :, yt].astype(f32) + hcore[yt].astype(f32)).astype(bf16)

        @pl.when(k < NY)
        def _():
            remote(hsum.at[yt], hy.at[y], hy_s.at[yt], hy_r.at[y], dp_of(yt), me).start()

        return 0

    lax.fori_loop(1, NY + 1, y_send, 0)
    ret[me] = cold_g[me]

    rows = oht.shape[0]
    slots_all = oht.shape[1]
    for r in range(0, rows, 128):
        ids = lax.broadcasted_iota(i32, (128, slots_all), 0) + r
        oht[pl.ds(r, 128), :] = (ids == asked_ref[...]).astype(f32).astype(bf16)
    hfin[...] = jnp.zeros_like(hfin)

    def y_wait(k, tot):
        ys = (y + k) % NY
        remote(hsum.at[ys], hy.at[ys], hy_s.at[ys], hy_r.at[ys], dp_of(ys), me).wait_recv()
        return 0

    lax.fori_loop(1, NY, y_wait, 0)
    hy[y] = hsum[y]
    tot = hy[0].astype(f32)
    for k in range(1, NY):
        tot = tot + hy[k].astype(f32)
    hz[...] = tot.astype(bf16)

    def t_send(k, _):
        p = peer(k, x, z)
        remote(hz.at[p], ht.at[me], ht_s.at[p], ht_r.at[me], dp, p).start()
        return 0

    lax.fori_loop(0, n - 1, t_send, 0)
    ht[me] = hz[me]

    def cold_wait(k, _):
        p = peer(k, x, z)
        remote(cold_g.at[p], ret.at[p], c_s.at[p], c_r.at[p], dp, p).wait_recv()
        return 0

    lax.fori_loop(0, n - 1, cold_wait, 0)
    width = ret.shape[2]
    back = ret[...].reshape(slots_all, width)

    def t_wait(k, _):
        p = peer(k, x, z)
        remote(hz.at[p], ht.at[p], ht_s.at[p], ht_r.at[p], dp, p).wait_recv()
        return 0

    lax.fori_loop(0, n - 1, t_wait, 0)
    hot_tot = jnp.sum(ht[...].astype(f32), axis=0)
    lanes = lax.broadcasted_iota(i32, (8, width), 1) // 128
    hot_tot = jnp.where(lanes == c, jnp.concatenate([hot_tot, hot_tot], axis=1), 0.0)
    hfin[pl.ds(0, 8), :] = hot_tot
    hot_rows = hfin[...].astype(bf16)
    blk = gl.shape[2]
    hot_ids = hot_pad_ref[y]

    def scatter(b, _):
        at = pl.ds(pl.multiple_of(b * blk, blk), blk)
        hot_sel = (lax.broadcasted_iota(i32, (blk, 128), 0) + b * blk == hot_ids).astype(f32).astype(bf16)
        g = jnp.dot(oht[at, :], back, preferred_element_type=f32)
        g = g + jnp.dot(hot_sel, hot_rows, preferred_element_type=f32)
        return g.astype(bf16)

    for q in range(NY):
        yt = (y + 1 + q) % NY
        gl[1 - c, yt] = scatter((1 - c) * NY + yt, 0)
        remote(gl.at[1 - c, yt], gcore.at[yt], gc_s.at[yt], gc_r.at[yt], partner, me).start()
    for q in range(NY):
        yt = (y + 1 + q) % NY
        gl[c, yt] = scatter(c * NY + yt, 0)
    for q in range(NY):
        yt = (y + 1 + q) % NY
        remote(gl.at[1 - c, yt], gcore.at[yt], gc_s.at[yt], gc_r.at[yt], partner, me).wait_recv()
        gsum[yt] = (gl[c, yt].astype(f32) + gcore[yt].astype(f32)).astype(bf16)
        if q < NY - 1:
            remote(gsum.at[yt], gy.at[y], gy_s.at[yt], gy_r.at[y], dp_of(yt), me).start()

    tot = gsum[y].astype(f32)
    for k in range(1, NY):
        ys = (y + k) % NY
        remote(gsum.at[ys], gy.at[ys], gy_s.at[ys], gy_r.at[ys], dp_of(ys), me).wait_recv()
        tot = tot + gy[ys].astype(f32)
    total_ref[c, y] = tot.astype(bf16)

    mine = total_ref.at[c, y]
    for k in range(1, NY):
        yt = (y + k) % NY
        remote(mine, mine, ag_s.at[yt], ag_r.at[y], dp_of(yt), me).start()
    remote(mine, mine, ac_s.at[y], ac_r.at[y], partner, me).start()

    def forward(k, _):
        ys = (y + k) % NY
        b = total_ref.at[c, ys]
        remote(b, b, ag_s.at[ys], ag_r.at[ys], dp_of(ys), me).wait_recv()
        remote(b, b, ac_s.at[ys], ac_r.at[ys], partner, me).start()
        return 0

    lax.fori_loop(1, NY, forward, 0)

    def finish_core(yt, _):
        b = total_ref.at[1 - c, yt]
        remote(b, b, ac_s.at[yt], ac_r.at[yt], partner, me).wait_recv()
        o = total_ref.at[c, yt]
        remote(o, o, ac_s.at[yt], ac_r.at[yt], partner, me).wait_send()
        remote(hot_g.at[1 - c, :, yt], hcore.at[yt], hc_s.at[yt], hc_r.at[yt], partner, me).wait_send()
        remote(gl.at[1 - c, yt], gcore.at[yt], gc_s.at[yt], gc_r.at[yt], partner, me).wait_send()
        return 0

    lax.fori_loop(0, NY, finish_core, 0)

    def finish_y(k, _):
        yt = (y + k) % NY
        remote(hsum.at[yt], hy.at[y], hy_s.at[yt], hy_r.at[y], dp_of(yt), me).wait_send()
        remote(gsum.at[yt], gy.at[y], gy_s.at[yt], gy_r.at[y], dp_of(yt), me).wait_send()
        remote(mine, mine, ag_s.at[yt], ag_r.at[y], dp_of(yt), me).wait_send()
        return 0

    lax.fori_loop(1, NY, finish_y, 0)

    def finish_t(k, _):
        p = peer(k, x, z)
        remote(cold_g.at[p], ret.at[me], c_s.at[p], c_r.at[me], dp, p).wait_send()
        remote(hz.at[p], ht.at[me], ht_s.at[p], ht_r.at[me], dp, p).wait_send()
        return 0

    lax.fori_loop(0, n - 1, finish_t, 0)


def reduce(hot_g, cold_g, asked, hot_ids, rows):
    n = NX * NZ
    slots, width = cold_g.shape[1:]
    blk = rows // (2 * NY)
    hot_pad = jnp.pad(hot_ids.reshape(NY, 8), ((0, 0), (0, 120)), constant_values=-1).reshape(NY, 1, 128)
    dma = pltpu.SemaphoreType.DMA
    vmem = pl.BlockSpec(memory_space=pltpu.VMEM)
    return pl.pallas_call(
        reduce_kernel,
        name="reduce",
        out_shape=jax.ShapeDtypeStruct((2, NY, blk, width), bf16),
        in_specs=[vmem] * 4,
        out_specs=vmem,
        scratch_shapes=[
            pltpu.VMEM((NY, n, 8, 128), bf16),
            pltpu.VMEM((NY, n, 8, 128), bf16),
            pltpu.VMEM((NY, n, 8, 128), bf16),
            pltpu.VMEM((n, 8, 128), bf16),
            pltpu.VMEM((n, 8, 128), bf16),
            pltpu.VMEM((n, slots, width), bf16),
            pltpu.VMEM((rows, n * slots), bf16),
            pltpu.VMEM((2, NY, blk, width), bf16),
            pltpu.VMEM((NY, blk, width), bf16),
            pltpu.VMEM((NY, blk, width), bf16),
            pltpu.VMEM((NY, blk, width), bf16),
            pltpu.VMEM((128, width), f32),
            dma((NY,)), dma((NY,)),
            dma((NY,)), dma((NY,)),
            dma((n,)), dma((n,)),
            dma((n,)), dma((n,)),
            dma((NY,)), dma((NY,)),
            dma((NY,)), dma((NY,)),
            dma((NY,)), dma((NY,)),
            dma((NY,)), dma((NY,)),
        ],
        compiler_params=pltpu.CompilerParams(
            collective_id=1, has_side_effects=True, vmem_limit_bytes=48 << 20
        ),
    )(hot_g.reshape(2, n, NY, 8, 128), cold_g, asked, hot_pad)


def adagrad_step(own_table, own_sum, grad):
    new_sum = own_sum + jnp.mean(grad * grad, axis=1)
    new_table = own_table - learning_rate * grad / jnp.sqrt(new_sum)[:, None]
    return (new_table, new_sum)


def per_device(bag_slots, labels, cold_ids, cold_count, table, adagrad_sum, hot_ids, w_in, w_out):
    n = NX * NZ
    rows, width = table.shape
    slots = cold_ids.shape[2]
    hot_rows, fetched, asked = fetch(table, hot_ids, cold_ids[0])
    live = (jnp.arange(slots, dtype=i32)[None, :] < cold_count[0][:, None]).astype(f32).reshape(1, n * slots)
    hot_g, cold_g = mlp(
        bag_slots, live, hot_rows.reshape(-1, width), fetched.reshape(-1, width), labels, w_in, w_out
    )
    asked_flat = asked[:, 0, :slots].reshape(1, n * slots)
    total = reduce(hot_g, cold_g.reshape(n, slots, width), asked_flat, hot_ids, rows)
    return adagrad_step(table, adagrad_sum, total.reshape(rows, width).astype(f32))


def solution(mesh):
    placed = (
        P(("dp", "table"), None),
        P(("dp", "table")),
        P(("dp", "table"), None, None),
        P(("dp", "table"), None),
        P("table", None),
        P("table"),
        P("table"),
        P(),
        P(),
    )
    return jax.shard_map(
        per_device,
        mesh=mesh,
        in_specs=placed,
        out_specs=(P("table", None), P("table")),
        check_vma=False,
    )
```

```python
import functools

import jax
import jax.numpy as jnp
from jax import lax
from jax.experimental import pallas as pl
from jax.experimental.pallas import tpu as pltpu
from jax.sharding import PartitionSpec as P

MESH = pl.DeviceIdType.MESH
learning_rate = 0.3
NX, NZ, NY = 4, 8, 8
bf16, f32, i32 = jnp.bfloat16, jnp.float32, jnp.int32


def remote(src, dst, send_sem, recv_sem, dp, table):
    return pltpu.make_async_remote_copy(
        src_ref=src,
        dst_ref=dst,
        send_sem=send_sem,
        recv_sem=recv_sem,
        device_id=(dp, table),
        device_id_type=MESH,
    )


def peer(k, x, z):
    m = k // NX
    kz = (NZ // 2 + (1 - 2 * (m % 2)) * ((m + 1) // 2)) % NZ
    kx = (k + 1) % NX
    return ((x + kx) % NX) * NZ + (z + kz) % NZ


def place():
    dp, me = lax.axis_index("dp"), lax.axis_index("table")
    y, c = dp // 2, dp % 2
    x, z = me // NZ, me % NZ
    partner = y * 2 + (1 - c)
    return dp, me, y, c, x, z, partner


def step_kernel(
    pre, mid,
    bag_ref, labels_ref, ids_ref, count_ref, table_hbm, sum_ref, hot_ids_ref, w_hbm, w_out_ref,
    table_out, sum_out,
    table_v, w_v, tb, ids3, asked, flat, hot_pad, bag_rows, bag2, sum_col,
    hot, fetched, oh, served, inc, wm, acc, dpool,
    hot_g, cold_g, hcore, hsum, hy, hz, ht, ret, oht, gacc, hfin, gl, gcore, gsum, gy, total,
    in_s, ids_s, ids_r, za_s, za_r, xb_s, xb_r, cc_s, cc_r, f_s, f_r,
    hc_s, hc_r, hy_s, hy_r, ht_s, ht_r, c_s, c_r, gc_s, gc_r, gy_s, gy_r, ag_s, ag_r, ac_s, ac_r,
):
    n = NX * NZ
    dp, me, y, c, x, z, partner = place()
    rows, width = table_v.shape
    slots = fetched.shape[1]
    half = hot.shape[3]
    hot_dev = 2 * half
    hot_cols = n * hot_dev
    per_y = hz.shape[1]
    batch, vocab = inc.shape
    parts = hc_s.shape[0]
    blk = gl.shape[2]

    def dp_of(yy):
        return yy * 2 + c

    def over(lo, hi, body):
        def run(k, _):
            body(k)
            return 0

        lax.fori_loop(lo, hi, run, 0)

    def eye(a, b, shift=0):
        return lax.broadcasted_iota(i32, (a, b), 0) + shift == lax.broadcasted_iota(i32, (a, b), 1)

    def to_column(mask, row):
        return jnp.sum(jnp.where(mask, row, 0.0), axis=1, keepdims=True)

    barrier = pltpu.get_barrier_semaphore()
    over(0, n - 1, lambda k: pl.semaphore_signal(
        barrier, inc=1, device_id=(dp, peer(k, x, z)), device_id_type=MESH))
    over(1, NY, lambda k: pl.semaphore_signal(
        barrier, inc=1, device_id=(dp_of((y + k) % NY), me), device_id_type=MESH))
    pl.semaphore_signal(barrier, inc=1, device_id=(partner, me), device_id_type=MESH)

    load_table = pltpu.make_async_copy(table_hbm, table_v, in_s.at[0])
    load_w = pltpu.make_async_copy(w_hbm, w_v, in_s.at[1])
    load_table.start()
    load_w.start()

    ids3[...] = jnp.full_like(ids3, -1)
    for t in range(n):
        ids3[t, :, pl.ds(0, slots)] = ids_ref[pl.ds(t, 1), :]
    hot_pad[...] = jnp.full_like(hot_pad, -1)
    hot_pad[:, pl.ds(0, hot_dev)] = hot_ids_ref[...]
    bag = bag_ref.shape[0]
    bag_rows[...] = bag_ref[...].T
    for s in range(8):
        bag2[:, pl.ds(s * bag, bag)] = bag_rows[pl.ds(s, batch // 8, stride=8), :]

    entries = 8 * bag
    tiles = vocab // 128
    own = lax.broadcasted_iota(i32, (8, entries), 1) // bag == lax.broadcasted_iota(i32, (8, entries), 0)
    tile_ids = lax.broadcasted_iota(i32, (tiles, 8, entries), 0)
    lane_ids = lax.broadcasted_iota(i32, (128, entries), 0)

    def build(i):
        outs = []
        for h in range(2):
            v = bag2[pl.ds(2 * i + h, 1), :]
            key = jnp.where(own, v >> 7, -1)
            left = (key[None] == tile_ids).astype(f32).reshape(tiles * 8, entries).astype(bf16)
            right = (lane_ids == (v & 127)).astype(f32).astype(bf16)
            outs.append(
                lax.dot_general(left, right, (((1,), (1,)), ((), ())), preferred_element_type=f32)
            )
        at = pl.ds(pl.multiple_of(16 * i, 16), 16)
        for k in range(tiles):
            t = jnp.concatenate([outs[0][8 * k : 8 * k + 8], outs[1][8 * k : 8 * k + 8]], axis=0)
            inc[at, pl.ds(k * 128, 128)] = t.astype(bf16)

    load_table.wait()
    tb[...] = table_v[...].astype(bf16)
    hot_col = to_column(eye(half, 128, c * half), hot_pad[...].astype(f32))
    hot_sel = (hot_col == lax.broadcasted_iota(i32, (half, rows), 1).astype(f32)).astype(f32).astype(bf16)
    hot[x, z, c] = jnp.dot(hot_sel, tb[...], preferred_element_type=f32).astype(bf16)
    asked[me] = ids3[me]
    over(0, pre, build)
    pl.semaphore_wait(barrier, n - 1 + NY)

    def send_ids(k):
        p = peer(k, x, z)
        remote(ids3.at[p], asked.at[me], ids_s.at[p], ids_r.at[me], dp, p).start()

    over(0, n - 1, send_ids)

    def hot_to_x(zs, xo):
        blk_ = hot.at[x, zs, c]
        remote(blk_, blk_, xb_s.at[xo, zs], xb_r.at[x, zs], dp, ((x + xo) % NX) * NZ + z).start()

    def hot_to_z(zo):
        blk_ = hot.at[x, z, c]
        remote(blk_, blk_, za_s.at[zo], za_r.at[z], dp, x * NZ + (z + zo) % NZ).start()

    over(1, NZ, hot_to_z)
    for xo in range(1, NX):
        hot_to_x(z, xo)
    over(pre, mid, build)

    def forward_x(zo):
        zs = (z + zo) % NZ
        blk_ = hot.at[x, zs, c]
        remote(blk_, blk_, za_s.at[zo], za_r.at[zs], dp, me).wait_recv()
        for xo in range(1, NX):
            hot_to_x(zs, xo)

    over(1, NZ, forward_x)
    line = hot.at[x, :, c]
    remote(line, line, cc_s.at[x], cc_r.at[x], partner, me).start()

    request = eye(slots, 128)
    chunk = served.shape[1] // slots

    def serve(ch):
        for j in range(chunk):
            k = ch * chunk + j
            p = peer(k, x, z)

            def arrived():
                remote(ids3.at[p], asked.at[p], ids_s.at[p], ids_r.at[p], dp, p).wait_recv()

            if j == chunk - 1:
                pl.when(k < n - 1)(arrived)
            else:
                arrived()
            col = to_column(request, asked[p].astype(f32))
            hit = col == lax.broadcasted_iota(i32, (slots, rows), 1).astype(f32)
            oh[pl.ds(j * slots, slots), :] = hit.astype(f32).astype(bf16)
        served[ch] = jnp.dot(oh[...], tb[...], preferred_element_type=f32).astype(bf16)
        for j in range(chunk):
            k = ch * chunk + j
            p = peer(k, x, z)
            block = served.at[ch, pl.ds(j * slots, slots)]

            def send():
                remote(block, fetched.at[me], f_s.at[p], f_r.at[me], dp, p).start()

            def keep():
                fetched[me] = served[ch, pl.ds(j * slots, slots)]

            if j == chunk - 1:
                pl.when(k < n - 1)(send)
                pl.when(k == n - 1)(keep)
            else:
                send()

    over(0, n // chunk, serve)
    over(mid, batch // 16, build)

    def line_to_partner(xo):
        xs = (x + xo) % NX

        def landed(zs):
            blk_ = hot.at[xs, zs, c]
            remote(blk_, blk_, xb_s.at[xo, zs], xb_r.at[xs, zs], dp, me).wait_recv()

        over(0, NZ, landed)
        line = hot.at[xs, :, c]
        remote(line, line, cc_s.at[xs], cc_r.at[xs], partner, me).start()

    over(1, NX, line_to_partner)

    for t in range(n):
        flat[:, pl.ds(t * slots, slots)] = asked[t][:, :slots]
    for b in range(rows // 128):
        sum_col[pl.ds(b * 128, 128), :] = to_column(eye(128, 128), sum_ref[pl.ds(b, 1), :])

    def finish_x(xs):
        line = hot.at[xs, :, 1 - c]
        remote(line, line, cc_s.at[xs], cc_r.at[xs], partner, me).wait_recv()

    over(0, NX, finish_x)
    acc[...] = jnp.dot(
        inc[:, pl.ds(0, hot_cols)], hot[...].reshape(hot_cols, width), preferred_element_type=f32
    )

    def fetched_wait(k):
        p = peer(k, x, z)
        remote(fetched.at[p], fetched.at[p], f_s.at[p], f_r.at[p], dp, p).wait_recv()

    over(0, n - 1, fetched_wait)
    slot_ids = lax.broadcasted_iota(i32, (slots, width), 0)

    def live(t):
        return slot_ids < count_ref[:, t : t + 1]

    for t in range(n):
        fetched[t] = jnp.where(live(t), fetched[t].astype(f32), 0.0).astype(bf16)
    pooled = (
        acc[...]
        + jnp.dot(
            inc[:, pl.ds(hot_cols, vocab - hot_cols)],
            fetched[...].reshape(n * slots, width),
            preferred_element_type=f32,
        )
    ).astype(bf16)

    load_w.wait()
    acc[...] = jnp.zeros_like(acc)
    hidden_units = w_v.shape[1]
    step = acc.shape[1]

    def forward(j):
        at = pl.ds(pl.multiple_of(j * step, step), step)
        pre_act = jnp.dot(pooled, w_v[:, at], preferred_element_type=f32)
        w = w_out_ref[:, at].astype(f32)
        acc[...] += jnp.maximum(pre_act, 0.0).astype(bf16).astype(f32) * w
        wm[:, at] = jnp.where(pre_act > 0, w, 0.0).astype(bf16)

    over(0, hidden_units // step, forward)
    logit = jnp.sum(acc[...], axis=1, keepdims=True)
    lab = jnp.concatenate(
        [to_column(eye(128, 128), labels_ref[:, pl.ds(b * 128, 128)]) for b in range(batch // 128)], axis=0
    )
    dlogit = jax.nn.sigmoid(logit) - lab
    dpool[...] = jnp.zeros_like(dpool)
    deep = min(1024, hidden_units)

    def backward(j):
        at = pl.ds(pl.multiple_of(j * deep, deep), deep)
        dhidden = (dlogit * wm[:, at].astype(f32)).astype(bf16)
        dpool[...] += lax.dot_general(
            dhidden, w_v[:, at], (((1,), (1,)), ((), ())), preferred_element_type=f32
        )

    over(0, hidden_units // deep, backward)
    dpooled = dpool[...].astype(bf16)

    def slot_grad(at, size):
        return lax.dot_general(
            inc[:, pl.ds(at, size)], dpooled, (((0,), (0,)), ((), ())), preferred_element_type=f32
        )

    def core_copy(q):
        at = pl.ds(q * (n // parts), n // parts)
        return remote(hot_g.at[1 - c, at], hcore.at[at], hc_s.at[q], hc_r.at[q], partner, me)

    owners = 256 // hot_dev
    for k in range(hot_cols // 256):
        g = slot_grad(k * 256, 256).reshape(owners, NY, per_y, width).astype(bf16)
        for h in range(2):
            hot_g[h, pl.ds(k * owners, owners)] = g[..., h * 128 : (h + 1) * 128]
        done = (k + 1) * parts
        if done % (hot_cols // 256) == 0:
            core_copy(done // (hot_cols // 256) - 1).start()
    cold_step = min(256, n * slots)
    for k in range(n * slots // cold_step):
        g = slot_grad(hot_cols + k * cold_step, cold_step)
        for i in range(cold_step // slots):
            t = k * (cold_step // slots) + i
            cold_g[t] = jnp.where(live(t), g[i * slots : (i + 1) * slots], 0.0).astype(bf16)

    def cold_send(k):
        p = peer(k, x, z)
        to = ret.at[pl.ds(pl.multiple_of(me * slots, slots), slots)]
        remote(cold_g.at[p], to, c_s.at[p], c_r.at[me], dp, p).start()

    def y_copy(src, yt, q):
        at = pl.ds(q * (n // parts), n // parts)
        return remote(hsum.at[yt, at], hy.at[src, at], hy_s.at[yt, q], hy_r.at[src, q], dp_of(yt), me)

    for q in range(parts):
        core_copy(q).wait_recv()
        at = pl.ds(q * (n // parts), n // parts)

        def y_send(k):
            yt = (y + k) % NY
            hsum[yt, at] = (hot_g[c, at, yt].astype(f32) + hcore[at, yt].astype(f32)).astype(bf16)

            @pl.when(k < NY)
            def _():
                y_copy(y, yt, q).start()

        over(1, NY + 1, y_send)
        if q == 0:
            over(0, n - 1, cold_send)
    ret[pl.ds(pl.multiple_of(me * slots, slots), slots), :] = cold_g[me]

    for r in range(0, rows, 128):
        ids = lax.broadcasted_iota(i32, (128, n * slots), 0) + r
        oht[pl.ds(r, 128), :] = (ids == flat[...]).astype(f32).astype(bf16)
    hfin[...] = jnp.zeros_like(hfin)

    def y_wait(k):
        ys = (y + k) % NY
        for q in range(parts):
            y_copy(ys, ys, q).wait_recv()

    over(1, NY, y_wait)
    hy[y] = hsum[y]
    tot = hy[0].astype(f32)
    for k in range(1, NY):
        tot = tot + hy[k].astype(f32)
    hz[...] = tot.astype(bf16)

    def t_send(k):
        p = peer(k, x, z)
        remote(hz.at[p], ht.at[me], ht_s.at[p], ht_r.at[me], dp, p).start()

    over(0, n - 1, t_send)
    ht[me] = hz[me]

    def cold_wait(k):
        p = peer(k, x, z)
        to = ret.at[pl.ds(pl.multiple_of(p * slots, slots), slots)]
        remote(cold_g.at[p], to, c_s.at[p], c_r.at[p], dp, p).wait_recv()

    over(0, n - 1, cold_wait)
    gacc[...] = jnp.dot(oht[...], ret[...], preferred_element_type=f32)

    def t_wait(k):
        p = peer(k, x, z)
        remote(hz.at[p], ht.at[p], ht_s.at[p], ht_r.at[p], dp, p).wait_recv()

    over(0, n - 1, t_wait)
    hot_tot = jnp.sum(ht[...].astype(f32), axis=0)
    lanes = lax.broadcasted_iota(i32, (per_y, width), 1) // 128
    hot_tot = jnp.where(lanes == c, jnp.concatenate([hot_tot, hot_tot], axis=1), 0.0)
    hfin[pl.ds(pl.multiple_of(y * per_y, 8), per_y), :] = hot_tot
    hot_rows = hfin[...].astype(bf16)

    def half_grad(cc):
        at = pl.ds(pl.multiple_of(cc * (rows // 2), 128), rows // 2)
        sel = (lax.broadcasted_iota(i32, (rows // 2, 128), 0) + cc * (rows // 2) == hot_pad[...]).astype(f32)
        g = gacc[at, :] + jnp.dot(sel.astype(bf16), hot_rows, preferred_element_type=f32)
        gl[cc] = g.astype(bf16).reshape(NY, blk, width)

    def g_core(yt):
        return remote(gl.at[1 - c, yt], gcore.at[yt], gc_s.at[yt], gc_r.at[yt], partner, me)

    def g_y(src, yt):
        return remote(gsum.at[yt], gy.at[src], gy_s.at[yt], gy_r.at[src], dp_of(yt), me)

    half_grad(1 - c)
    over(1, NY + 1, lambda k: g_core((y + k) % NY).start())
    half_grad(c)

    def g_send(k):
        yt = (y + k) % NY
        g_core(yt).wait_recv()
        gsum[yt] = (gl[c, yt].astype(f32) + gcore[yt].astype(f32)).astype(bf16)

        @pl.when(k < NY)
        def _():
            g_y(y, yt).start()

    over(1, NY + 1, g_send)
    tot = gsum[y].astype(f32)
    for k in range(1, NY):
        ys = (y + k) % NY
        g_y(ys, ys).wait_recv()
        tot = tot + gy[ys].astype(f32)
    total[c, y] = tot.astype(bf16)

    def to_y(src, yt):
        b = total.at[c, src]
        return remote(b, b, ag_s.at[yt], ag_r.at[src], dp_of(yt), me)

    def to_core(cc, yt):
        b = total.at[cc, yt]
        return remote(b, b, ac_s.at[yt], ac_r.at[yt], partner, me)

    over(1, NY, lambda k: to_y(y, (y + k) % NY).start())
    to_core(c, y).start()

    def update(cc, yy):
        at = pl.ds(pl.multiple_of((cc * NY + yy) * blk, blk), blk)
        g = total[cc, yy].astype(f32)
        new_sum = sum_col[at, :] + jnp.sum(g * g, axis=1, keepdims=True) * (1.0 / width)
        sum_col[at, :] = new_sum
        table_out[at, :] = table_v[at, :] - g * (learning_rate / jnp.sqrt(new_sum))

    update(c, y)

    def gather(k):
        ys = (y + k) % NY
        to_y(ys, ys).wait_recv()
        to_core(c, ys).start()
        update(c, ys)

    over(1, NY, gather)

    def gather_core(k):
        ys = (y + k) % NY
        to_core(1 - c, ys).wait_recv()
        update(1 - c, ys)

    over(0, NY, gather_core)
    for b in range(rows // 128):
        sum_out[pl.ds(b, 1), :] = jnp.sum(
            jnp.where(eye(128, 128), sum_col[pl.ds(b * 128, 128), :], 0.0), axis=0, keepdims=True
        )

    def finish_table(k):
        p = peer(k, x, z)
        remote(ids3.at[p], asked.at[me], ids_s.at[p], ids_r.at[me], dp, p).wait_send()
        remote(served.at[0, pl.ds(0, slots)], fetched.at[me], f_s.at[p], f_r.at[me], dp, p).wait_send()
        to = ret.at[pl.ds(pl.multiple_of(me * slots, slots), slots)]
        remote(cold_g.at[p], to, c_s.at[p], c_r.at[me], dp, p).wait_send()
        remote(hz.at[p], ht.at[me], ht_s.at[p], ht_r.at[me], dp, p).wait_send()

    over(0, n - 1, finish_table)

    def finish_hot(zo):
        blk_ = hot.at[x, z, c]

        @pl.when(zo > 0)
        def _():
            remote(blk_, blk_, za_s.at[zo], za_r.at[z], dp, me).wait_send()

        for xo in range(1, NX):
            remote(blk_, blk_, xb_s.at[xo, zo], xb_r.at[x, zo], dp, me).wait_send()

    over(0, NZ, finish_hot)

    def finish_line(xs):
        line = hot.at[xs, :, c]
        remote(line, line, cc_s.at[xs], cc_r.at[xs], partner, me).wait_send()

    over(0, NX, finish_line)
    for q in range(parts):
        core_copy(q).wait_send()

    def finish_y(k):
        yt = (y + k) % NY
        for q in range(parts):
            y_copy(y, yt, q).wait_send()
        g_y(y, yt).wait_send()
        to_y(y, yt).wait_send()

    over(1, NY, finish_y)

    def finish_core(yt):
        g_core(yt).wait_send()
        to_core(c, yt).wait_send()

    over(0, NY, finish_core)


def per_device(bag_slots, labels, cold_ids, cold_count, table, adagrad_sum, hot_ids, w_in, w_out):
    n = NX * NZ
    batch, bag = bag_slots.shape
    rows, width = table.shape
    slots = cold_ids.shape[2]
    hot_dev = hot_ids.shape[0]
    hot_cols = n * hot_dev
    vocab = n * (hot_dev + slots)
    hidden = w_in.shape[1]
    chunk = min(8, n)
    per_y = hot_dev // NY
    parts = 2 if hot_cols % 512 == 0 else 1
    blk = rows // (2 * NY)
    groups = batch // 16
    dma = pltpu.SemaphoreType.DMA
    vmem = pl.BlockSpec(memory_space=pltpu.VMEM)
    hbm = pl.BlockSpec(memory_space=pl.ANY)
    new_table, new_sum = pl.pallas_call(
        functools.partial(step_kernel, groups // 4, groups // 2),
        name="step",
        out_shape=(
            jax.ShapeDtypeStruct((rows, width), f32),
            jax.ShapeDtypeStruct((rows // 128, 128), f32),
        ),
        in_specs=[vmem, vmem, vmem, vmem, hbm, vmem, vmem, hbm, vmem],
        out_specs=(vmem, vmem),
        scratch_shapes=[
            pltpu.VMEM((rows, width), f32),
            pltpu.VMEM(w_in.shape, bf16),
            pltpu.VMEM((rows, width), bf16),
            pltpu.VMEM((n, 1, 128), i32),
            pltpu.VMEM((n, 1, 128), i32),
            pltpu.VMEM((1, n * slots), i32),
            pltpu.VMEM((1, 128), i32),
            pltpu.VMEM((batch, bag), i32),
            pltpu.VMEM((batch // 8, 8 * bag), i32),
            pltpu.VMEM((rows, 1), f32),
            pltpu.VMEM((NX, NZ, 2, hot_dev // 2, width), bf16),
            pltpu.VMEM((n, slots, width), bf16),
            pltpu.VMEM((chunk * slots, rows), bf16),
            pltpu.VMEM((n // chunk, chunk * slots, width), bf16),
            pltpu.VMEM((batch, vocab), bf16),
            pltpu.VMEM((batch, hidden), bf16),
            pltpu.VMEM((batch, 256), f32),
            pltpu.VMEM((batch, width), f32),
            pltpu.VMEM((2, n, NY, per_y, 128), bf16),
            pltpu.VMEM((n, slots, width), bf16),
            pltpu.VMEM((n, NY, per_y, 128), bf16),
            pltpu.VMEM((NY, n, per_y, 128), bf16),
            pltpu.VMEM((NY, n, per_y, 128), bf16),
            pltpu.VMEM((n, per_y, 128), bf16),
            pltpu.VMEM((n, per_y, 128), bf16),
            pltpu.VMEM((n * slots, width), bf16),
            pltpu.VMEM((rows, n * slots), bf16),
            pltpu.VMEM((rows, width), f32),
            pltpu.VMEM((128, width), f32),
            pltpu.VMEM((2, NY, blk, width), bf16),
            pltpu.VMEM((NY, blk, width), bf16),
            pltpu.VMEM((NY, blk, width), bf16),
            pltpu.VMEM((NY, blk, width), bf16),
            pltpu.VMEM((2, NY, blk, width), bf16),
            dma((2,)),
            dma((n,)), dma((n,)),
            dma((NZ,)), dma((NZ,)),
            dma((NX, NZ)), dma((NX, NZ)),
            dma((NX,)), dma((NX,)),
            dma((n,)), dma((n,)),
            dma((parts,)), dma((parts,)),
            dma((NY, parts)), dma((NY, parts)),
            dma((n,)), dma((n,)),
            dma((n,)), dma((n,)),
            dma((NY,)), dma((NY,)),
            dma((NY,)), dma((NY,)),
            dma((NY,)), dma((NY,)),
            dma((NY,)), dma((NY,)),
        ],
        compiler_params=pltpu.CompilerParams(
            collective_id=0, has_side_effects=True, vmem_limit_bytes=60 << 20
        ),
    )(
        bag_slots.T,
        labels.reshape(1, batch),
        cold_ids[0],
        cold_count,
        table,
        adagrad_sum.reshape(rows // 128, 128),
        hot_ids.reshape(1, hot_dev),
        w_in,
        w_out.reshape(1, hidden),
    )
    return new_table, new_sum.reshape(rows)


def solution(mesh):
    placed = (
        P(("dp", "table"), None),
        P(("dp", "table")),
        P(("dp", "table"), None, None),
        P(("dp", "table"), None),
        P("table", None),
        P("table"),
        P("table"),
        P(),
        P(),
    )
    return jax.shard_map(
        per_device,
        mesh=mesh,
        in_specs=placed,
        out_specs=(P("table", None), P("table")),
        check_vma=False,
    )
```

```python
import functools

import jax
import jax.numpy as jnp
from jax import lax
from jax.experimental import pallas as pl
from jax.experimental.pallas import tpu as pltpu
from jax.sharding import PartitionSpec as P

MESH = pl.DeviceIdType.MESH
learning_rate = 0.3
NX, NZ, NY = 4, 8, 8
bf16, f32, i32 = jnp.bfloat16, jnp.float32, jnp.int32


def remote(src, dst, send_sem, recv_sem, dp, table):
    return pltpu.make_async_remote_copy(
        src_ref=src,
        dst_ref=dst,
        send_sem=send_sem,
        recv_sem=recv_sem,
        device_id=(dp, table),
        device_id_type=MESH,
    )


def peer(k, x, z):
    m = k // NX
    kz = (NZ // 2 + (1 - 2 * (m % 2)) * ((m + 1) // 2)) % NZ
    kx = (k + 1) % NX
    return ((x + kx) % NX) * NZ + (z + kz) % NZ


def place():
    dp, me = lax.axis_index("dp"), lax.axis_index("table")
    y, c = dp // 2, dp % 2
    x, z = me // NZ, me % NZ
    partner = y * 2 + (1 - c)
    return dp, me, y, c, x, z, partner


def step_kernel(
    pre, mid,
    bag_ref, labels_ref, ids_ref, count_ref, table_hbm, sum_ref, hot_ids_ref, w_hbm, w_out_ref,
    table_out, sum_out,
    table_v, w_v, tb, ids3, asked, flat, hot_pad, bag_rows, bag2, sum_col,
    hot, fetched, oh, served, inc, wm, acc, dpool,
    hot_g, cold_g, hcore, hsum, hy, hz, ht, ret, oht, gacc, hfin, hsel, hotf, w_row, gl, gcore, gsum, gy, total,
    in_s, ids_s, ids_r, za_s, za_r, xb_s, xb_r, cc_s, cc_r, f_s, f_r,
    hc_s, hc_r, hy_s, hy_r, ht_s, ht_r, c_s, c_r, gc_s, gc_r, gy_s, gy_r, ag_s, ag_r, ac_s, ac_r, ha_s, ha_r,
):
    n = NX * NZ
    dp, me, y, c, x, z, partner = place()
    rows, width = table_v.shape
    slots = fetched.shape[1]
    half = hot.shape[3]
    hot_dev = 2 * half
    hot_cols = n * hot_dev
    per_y = hz.shape[1]
    batch, vocab = inc.shape
    parts = hc_s.shape[0]
    blk = gl.shape[2]

    def dp_of(yy):
        return yy * 2 + c

    def over(lo, hi, body, unroll=1):
        def run(k, _):
            body(k)
            return 0

        lax.fori_loop(lo, hi, run, 0, unroll=unroll)

    def eye(a, b, shift=0):
        return lax.broadcasted_iota(i32, (a, b), 0) + shift == lax.broadcasted_iota(i32, (a, b), 1)

    def to_column(mask, row):
        return jnp.sum(jnp.where(mask, row, 0.0), axis=1, keepdims=True)

    barrier = pltpu.get_barrier_semaphore()
    over(0, n - 1, lambda k: pl.semaphore_signal(
        barrier, inc=1, device_id=(dp, peer(k, x, z)), device_id_type=MESH))
    over(1, 2 * NY, lambda k: pl.semaphore_signal(
        barrier, inc=1, device_id=((dp + k) % (2 * NY), me), device_id_type=MESH))

    load_table = pltpu.make_async_copy(table_hbm, table_v, in_s.at[0])
    load_w = pltpu.make_async_copy(w_hbm, w_v, in_s.at[1])
    load_table.start()
    load_w.start()

    ids3[...] = jnp.full_like(ids3, -1)
    for t in range(n):
        ids3[t, :, pl.ds(0, slots)] = ids_ref[pl.ds(t, 1), :]
    hot_pad[...] = jnp.full_like(hot_pad, -1)
    hot_pad[:, pl.ds(0, hot_dev)] = hot_ids_ref[...]
    for k in range(w_out_ref.shape[0]):
        w_row[:, pl.ds(k * 128, 128)] = w_out_ref[pl.ds(k, 1), :].astype(f32)
    bag = bag_ref.shape[0]
    bag_rows[...] = bag_ref[...].T
    for s in range(8):
        bag2[:, pl.ds(s * bag, bag)] = bag_rows[pl.ds(s, batch // 8, stride=8), :]

    entries = 8 * bag
    tiles = vocab // 128
    own = lax.broadcasted_iota(i32, (8, entries), 1) // bag == lax.broadcasted_iota(i32, (8, entries), 0)
    tile_ids = lax.broadcasted_iota(i32, (tiles, 8, entries), 0)
    lane_ids = lax.broadcasted_iota(i32, (128, entries), 0)

    def build(i):
        outs = []
        for h in range(2):
            v = bag2[pl.ds(2 * i + h, 1), :]
            key = jnp.where(own, v >> 7, -1)
            left = (key[None] == tile_ids).astype(f32).reshape(tiles * 8, entries).astype(bf16)
            right = (lane_ids == (v & 127)).astype(f32).astype(bf16)
            outs.append(
                lax.dot_general(left, right, (((1,), (1,)), ((), ())), preferred_element_type=f32)
            )
        at = pl.ds(pl.multiple_of(16 * i, 16), 16)
        for k in range(tiles):
            t = jnp.concatenate([outs[0][8 * k : 8 * k + 8], outs[1][8 * k : 8 * k + 8]], axis=0)
            inc[at, pl.ds(k * 128, 128)] = t.astype(bf16)

    load_table.wait()
    tb[...] = table_v[...].astype(bf16)
    hot_col = to_column(eye(half, 128, c * half), hot_pad[...].astype(f32))
    hot_sel = (hot_col == lax.broadcasted_iota(i32, (half, rows), 1).astype(f32)).astype(f32).astype(bf16)
    hot[x, z, c] = jnp.dot(hot_sel, tb[...], preferred_element_type=f32).astype(bf16)
    asked[me] = ids3[me]
    over(0, pre, build)
    pl.semaphore_wait(barrier, n - 1 + 2 * NY - 1)

    def send_ids(k):
        p = peer(k, x, z)
        remote(ids3.at[p], asked.at[me], ids_s.at[p], ids_r.at[me], dp, p).start()

    over(0, n - 1, send_ids)

    def hot_to_x(zs, xo):
        blk_ = hot.at[x, zs, c]
        remote(blk_, blk_, xb_s.at[xo, zs], xb_r.at[x, zs], dp, ((x + xo) % NX) * NZ + z).start()

    def hot_to_z(zo):
        blk_ = hot.at[x, z, c]
        remote(blk_, blk_, za_s.at[zo], za_r.at[z], dp, x * NZ + (z + zo) % NZ).start()

    over(1, NZ, hot_to_z)
    for xo in range(1, NX):
        hot_to_x(z, xo)
    over(pre, mid, build)

    def forward_x(zo):
        zs = (z + zo) % NZ
        blk_ = hot.at[x, zs, c]
        remote(blk_, blk_, za_s.at[zo], za_r.at[zs], dp, me).wait_recv()
        for xo in range(1, NX):
            hot_to_x(zs, xo)

    over(1, NZ, forward_x)
    line = hot.at[x, :, c]
    remote(line, line, cc_s.at[x], cc_r.at[x], partner, me).start()

    request = eye(slots, 128)
    chunk = served.shape[1] // slots

    def serve(ch):
        for j in range(chunk):
            k = ch * chunk + j
            p = peer((2 * n - 2 - k) % n, x, z)

            def arrived():
                remote(ids3.at[p], asked.at[p], ids_s.at[p], ids_r.at[p], dp, p).wait_recv()

            if j == chunk - 1:
                pl.when(k < n - 1)(arrived)
            else:
                arrived()
            col = to_column(request, asked[p].astype(f32))
            hit = col == lax.broadcasted_iota(i32, (slots, rows), 1).astype(f32)
            oh[pl.ds(j * slots, slots), :] = hit.astype(f32).astype(bf16)
        served[ch] = jnp.dot(oh[...], tb[...], preferred_element_type=f32).astype(bf16)
        for j in range(chunk):
            k = ch * chunk + j
            p = peer((2 * n - 2 - k) % n, x, z)
            block = served.at[ch, pl.ds(j * slots, slots)]

            def send():
                remote(block, fetched.at[me], f_s.at[p], f_r.at[me], dp, p).start()

            def keep():
                fetched[me] = served[ch, pl.ds(j * slots, slots)]

            if j == chunk - 1:
                pl.when(k < n - 1)(send)
                pl.when(k == n - 1)(keep)
            else:
                send()

    over(0, n // chunk, serve)
    over(mid, batch // 16, build)

    def line_to_partner(xo):
        xs = (x + xo) % NX

        def landed(zs):
            blk_ = hot.at[xs, zs, c]
            remote(blk_, blk_, xb_s.at[xo, zs], xb_r.at[xs, zs], dp, me).wait_recv()

        over(0, NZ, landed)
        line = hot.at[xs, :, c]
        remote(line, line, cc_s.at[xs], cc_r.at[xs], partner, me).start()

    over(1, NX, line_to_partner)

    for t in range(n):
        flat[:, pl.ds(t * slots, slots)] = asked[t][:, :slots]
    for b in range(rows // 128):
        sum_col[pl.ds(b * 128, 128), :] = to_column(eye(128, 128), sum_ref[pl.ds(b, 1), :])

    def finish_x(xs):
        line = hot.at[xs, :, 1 - c]
        remote(line, line, cc_s.at[xs], cc_r.at[xs], partner, me).wait_recv()

    over(0, NX, finish_x)
    acc[...] = jnp.dot(
        inc[:, pl.ds(0, hot_cols)], hot[...].reshape(hot_cols, width), preferred_element_type=f32
    )

    def fetched_wait(k):
        p = peer(k, x, z)
        remote(fetched.at[p], fetched.at[p], f_s.at[p], f_r.at[p], dp, p).wait_recv()

    over(0, n - 1, fetched_wait)
    slot_ids = lax.broadcasted_iota(i32, (slots, width), 0)

    def live(t):
        return slot_ids < count_ref[:, t : t + 1]

    for t in range(n):
        fetched[t] = jnp.where(live(t), fetched[t].astype(f32), 0.0).astype(bf16)
    pooled = (
        acc[...]
        + jnp.dot(
            inc[:, pl.ds(hot_cols, vocab - hot_cols)],
            fetched[...].reshape(n * slots, width),
            preferred_element_type=f32,
        )
    ).astype(bf16)

    load_w.wait()
    acc[...] = jnp.zeros_like(acc)
    hidden_units = w_v.shape[1]
    step = acc.shape[1]

    def forward(j):
        at = pl.ds(pl.multiple_of(j * step, step), step)
        pre_act = jnp.dot(pooled, w_v[:, at], preferred_element_type=f32)
        w = w_row[:, at]
        acc[...] += jnp.maximum(pre_act, 0.0).astype(bf16).astype(f32) * w
        wm[:, at] = jnp.where(pre_act > 0, w, 0.0).astype(bf16)

    over(0, hidden_units // step, forward, unroll=2)
    logit = jnp.sum(acc[...], axis=1, keepdims=True)
    lab = jnp.concatenate(
        [to_column(eye(128, 128), labels_ref[:, pl.ds(b * 128, 128)]) for b in range(batch // 128)], axis=0
    )
    dlogit = jax.nn.sigmoid(logit) - lab
    dpool[...] = jnp.zeros_like(dpool)
    deep = min(1024, hidden_units)

    def backward(j):
        at = pl.ds(pl.multiple_of(j * deep, deep), deep)
        dhidden = (dlogit * wm[:, at].astype(f32)).astype(bf16)
        dpool[...] += lax.dot_general(
            dhidden, w_v[:, at], (((1,), (1,)), ((), ())), preferred_element_type=f32
        )

    over(0, hidden_units // deep, backward)
    dpooled = dpool[...].astype(bf16)

    def slot_grad(at, size):
        return lax.dot_general(
            inc[:, pl.ds(at, size)], dpooled, (((0,), (0,)), ((), ())), preferred_element_type=f32
        )

    def core_copy(q):
        at = pl.ds(q * (n // parts), n // parts)
        return remote(hot_g.at[1 - c, at], hcore.at[at], hc_s.at[q], hc_r.at[q], partner, me)

    cold_step = min(256, n * slots)
    for k in range(n * slots // cold_step):
        g = slot_grad(hot_cols + k * cold_step, cold_step)
        for i in range(cold_step // slots):
            t = k * (cold_step // slots) + i
            cold_g[t] = jnp.where(live(t), g[i * slots : (i + 1) * slots], 0.0).astype(bf16)

    def cold_send(k):
        p = peer(k, x, z)
        to = ret.at[pl.ds(pl.multiple_of(me * slots, slots), slots)]
        remote(cold_g.at[p], to, c_s.at[p], c_r.at[me], dp, p).start()

    over(0, n - 1, cold_send)
    owners = 256 // hot_dev
    for k in range(hot_cols // 256):
        g = slot_grad(k * 256, 256).reshape(owners, NY, per_y, width).astype(bf16)
        for h in range(2):
            hot_g[h, pl.ds(k * owners, owners)] = g[..., h * 128 : (h + 1) * 128]
        done = (k + 1) * parts
        if done % (hot_cols // 256) == 0:
            core_copy(done // (hot_cols // 256) - 1).start()

    def y_copy(src, yt, q):
        at = pl.ds(q * (n // parts), n // parts)
        return remote(hsum.at[yt, at], hy.at[src, at], hy_s.at[yt, q], hy_r.at[src, q], dp_of(yt), me)

    for r in range(0, rows, 128):
        ids = lax.broadcasted_iota(i32, (128, n * slots), 0) + r
        oht[pl.ds(r, 128), :] = (ids == flat[...]).astype(f32).astype(bf16)
    for q in range(parts):
        core_copy(q).wait_recv()
        at = pl.ds(q * (n // parts), n // parts)

        def y_send(k):
            yt = (y + k) % NY
            hsum[yt, at] = (hot_g[c, at, yt].astype(f32) + hcore[at, yt].astype(f32)).astype(bf16)

            @pl.when(k < NY)
            def _():
                y_copy(y, yt, q).start()

        over(1, NY + 1, y_send)
    ret[pl.ds(pl.multiple_of(me * slots, slots), slots), :] = cold_g[me]
    hsel[...] = (lax.broadcasted_iota(i32, (rows, 128), 0) == hot_pad[...]).astype(f32).astype(bf16)
    hfin[...] = jnp.zeros_like(hfin)

    def cold_wait(k):
        p = peer(k, x, z)
        to = ret.at[pl.ds(pl.multiple_of(p * slots, slots), slots)]
        remote(cold_g.at[p], to, c_s.at[p], c_r.at[p], dp, p).wait_recv()

    over(0, n - 1, cold_wait)

    def half_grad(cc):
        at = pl.ds(pl.multiple_of(cc * (rows // 2), 128), rows // 2)
        g = jnp.dot(oht[at, :], ret[...], preferred_element_type=f32)
        gl[cc] = g.astype(bf16).reshape(NY, blk, width)

    def g_core(yt):
        return remote(gl.at[1 - c, yt], gcore.at[yt], gc_s.at[yt], gc_r.at[yt], partner, me)

    def g_y(src, yt):
        return remote(gsum.at[yt], gy.at[src], gy_s.at[yt], gy_r.at[src], dp_of(yt), me)

    half_grad(1 - c)
    over(1, NY + 1, lambda k: g_core((y + k) % NY).start())
    half_grad(c)

    def g_send(k):
        yt = (y + k) % NY
        g_core(yt).wait_recv()
        gsum[yt] = (gl[c, yt].astype(f32) + gcore[yt].astype(f32)).astype(bf16)

        @pl.when(k < NY)
        def _():
            g_y(y, yt).start()

    over(1, NY + 1, g_send)

    def y_wait(k):
        ys = (y + k) % NY
        for q in range(parts):
            y_copy(ys, ys, q).wait_recv()

    over(1, NY, y_wait)
    hy[y] = hsum[y]
    tot = hy[0].astype(f32)
    for k in range(1, NY):
        tot = tot + hy[k].astype(f32)
    hz[...] = tot.astype(bf16)

    def t_send(k):
        p = peer(k, x, z)
        remote(hz.at[p], ht.at[me], ht_s.at[p], ht_r.at[me], dp, p).start()

    over(0, n - 1, t_send)
    ht[me] = hz[me]

    tot = gsum[y].astype(f32)
    for k in range(1, NY):
        ys = (y + k) % NY
        g_y(ys, ys).wait_recv()
        tot = tot + gy[ys].astype(f32)
    total[c, y] = tot.astype(bf16)

    def to_y(src, yt):
        b = total.at[c, src]
        return remote(b, b, ag_s.at[yt], ag_r.at[src], dp_of(yt), me)

    def to_core(cc, yt):
        b = total.at[cc, yt]
        return remote(b, b, ac_s.at[yt], ac_r.at[yt], partner, me)

    over(1, NY, lambda k: to_y(y, (y + k) % NY).start())
    to_core(c, y).start()

    def t_wait(k):
        p = peer(k, x, z)
        remote(hz.at[p], ht.at[p], ht_s.at[p], ht_r.at[p], dp, p).wait_recv()

    over(0, n - 1, t_wait)
    hotf[c, pl.ds(pl.multiple_of(y * per_y, 8), per_y), :] = jnp.sum(ht[...].astype(f32), axis=0)

    def h_copy(src, to):
        b = hotf.at[src % 2, pl.ds(pl.multiple_of(src // 2 * per_y, 8), per_y)]
        return remote(b, b, ha_s.at[to], ha_r.at[src], to, me)

    over(1, 2 * NY, lambda k: h_copy(dp, (dp + k) % (2 * NY)).start())

    def h_wait(k):
        src = (dp + k) % (2 * NY)
        h_copy(src, src).wait_recv()

    over(1, 2 * NY, h_wait)
    for h in range(2):
        hfin[pl.ds(0, hot_dev), pl.ds(h * 128, 128)] = hotf[h]
    gacc[...] = jnp.dot(hsel[...], hfin[...].astype(bf16), preferred_element_type=f32)

    def update(cc, yy):
        at = pl.ds(pl.multiple_of((cc * NY + yy) * blk, blk), blk)
        g = total[cc, yy].astype(f32) + gacc[at, :]
        new_sum = sum_col[at, :] + jnp.sum(g * g, axis=1, keepdims=True) * (1.0 / width)
        sum_col[at, :] = new_sum
        table_out[at, :] = table_v[at, :] - g * (learning_rate / jnp.sqrt(new_sum))

    update(c, y)

    def gather(k):
        ys = (y + k) % NY
        to_y(ys, ys).wait_recv()
        to_core(c, ys).start()
        update(c, ys)

    over(1, NY, gather)

    def gather_core(k):
        ys = (y + k) % NY
        to_core(1 - c, ys).wait_recv()
        update(1 - c, ys)

    over(0, NY, gather_core)
    for b in range(rows // 128):
        sum_out[pl.ds(b, 1), :] = jnp.sum(
            jnp.where(eye(128, 128), sum_col[pl.ds(b * 128, 128), :], 0.0), axis=0, keepdims=True
        )

    def finish_table(k):
        p = peer(k, x, z)
        remote(ids3.at[p], asked.at[me], ids_s.at[p], ids_r.at[me], dp, p).wait_send()
        remote(served.at[0, pl.ds(0, slots)], fetched.at[me], f_s.at[p], f_r.at[me], dp, p).wait_send()
        to = ret.at[pl.ds(pl.multiple_of(me * slots, slots), slots)]
        remote(cold_g.at[p], to, c_s.at[p], c_r.at[me], dp, p).wait_send()
        remote(hz.at[p], ht.at[me], ht_s.at[p], ht_r.at[me], dp, p).wait_send()

    over(0, n - 1, finish_table)

    def finish_hot(zo):
        blk_ = hot.at[x, z, c]

        @pl.when(zo > 0)
        def _():
            remote(blk_, blk_, za_s.at[zo], za_r.at[z], dp, me).wait_send()

        for xo in range(1, NX):
            remote(blk_, blk_, xb_s.at[xo, zo], xb_r.at[x, zo], dp, me).wait_send()

    over(0, NZ, finish_hot)

    def finish_line(xs):
        line = hot.at[xs, :, c]
        remote(line, line, cc_s.at[xs], cc_r.at[xs], partner, me).wait_send()

    over(0, NX, finish_line)
    for q in range(parts):
        core_copy(q).wait_send()

    def finish_y(k):
        yt = (y + k) % NY
        for q in range(parts):
            y_copy(y, yt, q).wait_send()
        g_y(y, yt).wait_send()
        to_y(y, yt).wait_send()

    over(1, NY, finish_y)
    over(1, 2 * NY, lambda k: h_copy(dp, (dp + k) % (2 * NY)).wait_send())

    def finish_core(yt):
        g_core(yt).wait_send()
        to_core(c, yt).wait_send()

    over(0, NY, finish_core)


def emit_kernel(table_ref, sum_ref, table_out, sum_out, sems):
    copies = [
        pltpu.make_async_copy(table_ref, table_out, sems.at[0]),
        pltpu.make_async_copy(sum_ref, sum_out, sems.at[1]),
    ]
    for copy in copies:
        copy.start()
    for copy in copies:
        copy.wait()


def per_device(bag_slots, labels, cold_ids, cold_count, table, adagrad_sum, hot_ids, w_in, w_out):
    n = NX * NZ
    batch, bag = bag_slots.shape
    rows, width = table.shape
    slots = cold_ids.shape[2]
    hot_dev = hot_ids.shape[0]
    hot_cols = n * hot_dev
    vocab = n * (hot_dev + slots)
    hidden = w_in.shape[1]
    chunk = min(8, n)
    per_y = hot_dev // NY
    parts = 2 if hot_cols % 512 == 0 else 1
    blk = rows // (2 * NY)
    groups = batch // 16
    dma = pltpu.SemaphoreType.DMA
    vmem = pl.BlockSpec(memory_space=pltpu.VMEM)
    hbm = pl.BlockSpec(memory_space=pl.ANY)
    new_table, new_sum = pl.pallas_call(
        functools.partial(step_kernel, groups // 4, groups // 2),
        name="step",
        out_shape=(
            jax.ShapeDtypeStruct((rows, width), f32),
            jax.ShapeDtypeStruct((rows // 128, 128), f32),
        ),
        in_specs=[vmem, vmem, vmem, vmem, hbm, vmem, vmem, hbm, vmem],
        out_specs=(vmem, vmem),
        scratch_shapes=[
            pltpu.VMEM((rows, width), f32),
            pltpu.VMEM(w_in.shape, bf16),
            pltpu.VMEM((rows, width), bf16),
            pltpu.VMEM((n, 1, 128), i32),
            pltpu.VMEM((n, 1, 128), i32),
            pltpu.VMEM((1, n * slots), i32),
            pltpu.VMEM((1, 128), i32),
            pltpu.VMEM((batch, bag), i32),
            pltpu.VMEM((batch // 8, 8 * bag), i32),
            pltpu.VMEM((rows, 1), f32),
            pltpu.VMEM((NX, NZ, 2, hot_dev // 2, width), bf16),
            pltpu.VMEM((n, slots, width), bf16),
            pltpu.VMEM((chunk * slots, rows), bf16),
            pltpu.VMEM((n // chunk, chunk * slots, width), bf16),
            pltpu.VMEM((batch, vocab), bf16),
            pltpu.VMEM((batch, hidden), bf16),
            pltpu.VMEM((batch, 256), f32),
            pltpu.VMEM((batch, width), f32),
            pltpu.VMEM((2, n, NY, per_y, 128), bf16),
            pltpu.VMEM((n, slots, width), bf16),
            pltpu.VMEM((n, NY, per_y, 128), bf16),
            pltpu.VMEM((NY, n, per_y, 128), bf16),
            pltpu.VMEM((NY, n, per_y, 128), bf16),
            pltpu.VMEM((n, per_y, 128), bf16),
            pltpu.VMEM((n, per_y, 128), bf16),
            pltpu.VMEM((n * slots, width), bf16),
            pltpu.VMEM((rows, n * slots), bf16),
            pltpu.VMEM((rows, width), f32),
            pltpu.VMEM((128, width), f32),
            pltpu.VMEM((rows, 128), bf16),
            pltpu.VMEM((2, hot_dev, 128), f32),
            pltpu.VMEM((1, hidden), f32),
            pltpu.VMEM((2, NY, blk, width), bf16),
            pltpu.VMEM((NY, blk, width), bf16),
            pltpu.VMEM((NY, blk, width), bf16),
            pltpu.VMEM((NY, blk, width), bf16),
            pltpu.VMEM((2, NY, blk, width), bf16),
            dma((2,)),
            dma((n,)), dma((n,)),
            dma((NZ,)), dma((NZ,)),
            dma((NX, NZ)), dma((NX, NZ)),
            dma((NX,)), dma((NX,)),
            dma((n,)), dma((n,)),
            dma((parts,)), dma((parts,)),
            dma((NY, parts)), dma((NY, parts)),
            dma((n,)), dma((n,)),
            dma((n,)), dma((n,)),
            dma((NY,)), dma((NY,)),
            dma((NY,)), dma((NY,)),
            dma((NY,)), dma((NY,)),
            dma((NY,)), dma((NY,)),
            dma((2 * NY,)), dma((2 * NY,)),
        ],
        compiler_params=pltpu.CompilerParams(
            collective_id=0, has_side_effects=True, vmem_limit_bytes=60 << 20
        ),
    )(
        bag_slots.T,
        labels.reshape(1, batch),
        cold_ids[0],
        cold_count,
        table,
        adagrad_sum.reshape(rows // 128, 128),
        hot_ids.reshape(1, hot_dev),
        w_in,
        w_out.reshape(hidden // 128, 128),
    )
    out_table, out_sum = pl.pallas_call(
        emit_kernel,
        name="emit",
        out_shape=(
            jax.ShapeDtypeStruct((rows, width), f32),
            jax.ShapeDtypeStruct((rows // 128, 128), f32),
        ),
        in_specs=[vmem, vmem],
        out_specs=(hbm, hbm),
        scratch_shapes=[dma((2,))],
    )(new_table, new_sum)
    return out_table, out_sum.reshape(rows)


def solution(mesh):
    placed = (
        P(("dp", "table"), None),
        P(("dp", "table")),
        P(("dp", "table"), None, None),
        P(("dp", "table"), None),
        P("table", None),
        P("table"),
        P("table"),
        P(),
        P(),
    )
    return jax.shard_map(
        per_device,
        mesh=mesh,
        in_specs=placed,
        out_specs=(P("table", None), P("table")),
        check_vma=False,
    )
```

```python
import functools

import jax
import jax.numpy as jnp
from jax import lax
from jax.experimental import pallas as pl
from jax.experimental.pallas import tpu as pltpu
from jax.sharding import PartitionSpec as P

MESH = pl.DeviceIdType.MESH
learning_rate = 0.3
NX, NZ, NY = 4, 8, 8
bf16, f32, i32 = jnp.bfloat16, jnp.float32, jnp.int32


def remote(src, dst, send_sem, recv_sem, dp, table):
    return pltpu.make_async_remote_copy(
        src_ref=src,
        dst_ref=dst,
        send_sem=send_sem,
        recv_sem=recv_sem,
        device_id=(dp, table),
        device_id_type=MESH,
    )


def peer(k, x, z):
    m = k // NX
    kz = (NZ // 2 + (1 - 2 * (m % 2)) * ((m + 1) // 2)) % NZ
    kx = (k + 1) % NX
    return ((x + kx) % NX) * NZ + (z + kz) % NZ


def y_peer(k, y):
    return (y + NY // 2 + (1 - 2 * (k % 2)) * ((k + 1) // 2)) % NY


def place():
    dp, me = lax.axis_index("dp"), lax.axis_index("table")
    y, c = dp // 2, dp % 2
    x, z = me // NZ, me % NZ
    partner = y * 2 + (1 - c)
    return dp, me, y, c, x, z, partner


def step_kernel(
    pre, mid,
    table_hbm, w_hbm, bag_hbm, labels_hbm, ids_hbm, count_hbm, sum_hbm, hot_ids_hbm, w_out_hbm,
    table_out, sum_out,
    bag_ref, labels_ref, ids_ref, count_ref, sum_ref, hot_ids_ref, w_out_ref,
    table_v, w_v, tb, ids3, asked, flat, hot_pad, bag_rows, bag2, sum_col,
    hot, fetched, oh, served, inc, wm, acc, dpool,
    hot_g, cold_g, hcore, hsum, hy, hz, ht, ret, oht, gacc, hfin, hsel, hotf, w_row, gl, gcore, gsum, gy, total, new_rows,
    in_s, out_s, ids_s, ids_r, za_s, za_r, xb_s, xb_r, cc_s, cc_r, f_s, f_r,
    hc_s, hc_r, hy_s, hy_r, ht_s, ht_r, c_s, c_r, gc_s, gc_r, gy_s, gy_r, ag_s, ag_r, ac_s, ac_r, ha_s, ha_r,
):
    n = NX * NZ
    dp, me, y, c, x, z, partner = place()
    rows, width = table_v.shape
    slots = fetched.shape[1]
    half = hot.shape[3]
    hot_dev = 2 * half
    hot_cols = n * hot_dev
    per_y = hz.shape[1]
    batch, vocab = inc.shape
    parts = hc_s.shape[0]
    subs, sub = gl.shape[1], gl.shape[3]

    def dp_of(yy):
        return yy * 2 + c

    def over(lo, hi, body, unroll=1):
        def run(k, _):
            body(k)
            return 0

        lax.fori_loop(lo, hi, run, 0, unroll=unroll)

    def eye(a, b, shift=0):
        return lax.broadcasted_iota(i32, (a, b), 0) + shift == lax.broadcasted_iota(i32, (a, b), 1)

    def to_column(mask, row):
        return jnp.sum(jnp.where(mask, row, 0.0), axis=1, keepdims=True)

    barrier = pltpu.get_barrier_semaphore()
    over(0, n - 1, lambda k: pl.semaphore_signal(
        barrier, inc=1, device_id=(dp, peer(k, x, z)), device_id_type=MESH))
    over(1, 2 * NY, lambda k: pl.semaphore_signal(
        barrier, inc=1, device_id=((dp + k) % (2 * NY), me), device_id_type=MESH))

    small = (
        (ids_hbm, ids_ref), (hot_ids_hbm, hot_ids_ref), (bag_hbm, bag_ref), (w_out_hbm, w_out_ref),
        (count_hbm, count_ref), (sum_hbm, sum_ref), (labels_hbm, labels_ref),
    )
    loads = [pltpu.make_async_copy(a, b, in_s.at[i + 2]) for i, (a, b) in enumerate(small)]
    load_table = pltpu.make_async_copy(table_hbm, table_v, in_s.at[0])
    load_w = pltpu.make_async_copy(w_hbm, w_v, in_s.at[1])
    for load in loads[:2]:
        load.start()
    load_table.start()
    for load in loads[2:]:
        load.start()
    load_w.start()
    for load in loads:
        load.wait()

    ids3[...] = jnp.full_like(ids3, -1)
    for t in range(n):
        ids3[t, :, pl.ds(0, slots)] = ids_ref[pl.ds(t, 1), :]
    hot_pad[...] = jnp.full_like(hot_pad, -1)
    hot_pad[:, pl.ds(0, hot_dev)] = hot_ids_ref[...]
    for k in range(w_out_ref.shape[0]):
        w_row[:, pl.ds(k * 128, 128)] = w_out_ref[pl.ds(k, 1), :].astype(f32)
    bag = bag_ref.shape[0]
    bag_rows[...] = bag_ref[...].T
    for s in range(8):
        bag2[:, pl.ds(s * bag, bag)] = bag_rows[pl.ds(s, batch // 8, stride=8), :]

    entries = 8 * bag
    tiles = vocab // 128
    own = lax.broadcasted_iota(i32, (8, entries), 1) // bag == lax.broadcasted_iota(i32, (8, entries), 0)
    tile_ids = lax.broadcasted_iota(i32, (tiles, 8, entries), 0)
    lane_ids = lax.broadcasted_iota(i32, (128, entries), 0)

    def build(i):
        outs = []
        for h in range(2):
            v = bag2[pl.ds(2 * i + h, 1), :]
            key = jnp.where(own, v >> 7, -1)
            left = (key[None] == tile_ids).astype(f32).reshape(tiles * 8, entries).astype(bf16)
            right = (lane_ids == (v & 127)).astype(f32).astype(bf16)
            outs.append(
                lax.dot_general(left, right, (((1,), (1,)), ((), ())), preferred_element_type=f32)
            )
        at = pl.ds(pl.multiple_of(16 * i, 16), 16)
        for k in range(tiles):
            t = jnp.concatenate([outs[0][8 * k : 8 * k + 8], outs[1][8 * k : 8 * k + 8]], axis=0)
            inc[at, pl.ds(k * 128, 128)] = t.astype(bf16)

    load_table.wait()
    tb[...] = table_v[...].astype(bf16)
    hot_col = to_column(eye(half, 128, c * half), hot_pad[...].astype(f32))
    hot_sel = (hot_col == lax.broadcasted_iota(i32, (half, rows), 1).astype(f32)).astype(f32).astype(bf16)
    hot[x, z, c] = jnp.dot(hot_sel, tb[...], preferred_element_type=f32).astype(bf16)
    asked[me] = ids3[me]
    over(0, pre, build)
    pl.semaphore_wait(barrier, n - 1 + 2 * NY - 1)

    def send_ids(k):
        p = peer(k, x, z)
        remote(ids3.at[p], asked.at[me], ids_s.at[p], ids_r.at[me], dp, p).start()

    over(0, n - 1, send_ids)

    def hot_to_x(zs, xo):
        blk_ = hot.at[x, zs, c]
        remote(blk_, blk_, xb_s.at[xo, zs], xb_r.at[x, zs], dp, ((x + xo) % NX) * NZ + z).start()

    def hot_to_z(zo):
        blk_ = hot.at[x, z, c]
        remote(blk_, blk_, za_s.at[zo], za_r.at[z], dp, x * NZ + (z + zo) % NZ).start()

    over(1, NZ, hot_to_z)
    for xo in range(1, NX):
        hot_to_x(z, xo)
    over(pre, mid, build)

    def forward_x(zo):
        zs = (z + zo) % NZ
        blk_ = hot.at[x, zs, c]
        remote(blk_, blk_, za_s.at[zo], za_r.at[zs], dp, me).wait_recv()
        for xo in range(1, NX):
            hot_to_x(zs, xo)

    over(1, NZ, forward_x)
    line = hot.at[x, :, c]
    remote(line, line, cc_s.at[x], cc_r.at[x], partner, me).start()

    request = eye(slots, 128)
    chunk = served.shape[1] // slots

    def serve(ch):
        for j in range(chunk):
            k = ch * chunk + j
            p = peer((2 * n - 2 - k) % n, x, z)

            def arrived():
                remote(ids3.at[p], asked.at[p], ids_s.at[p], ids_r.at[p], dp, p).wait_recv()

            if j == chunk - 1:
                pl.when(k < n - 1)(arrived)
            else:
                arrived()
            col = to_column(request, asked[p].astype(f32))
            hit = col == lax.broadcasted_iota(i32, (slots, rows), 1).astype(f32)
            oh[pl.ds(j * slots, slots), :] = hit.astype(f32).astype(bf16)
        served[ch] = jnp.dot(oh[...], tb[...], preferred_element_type=f32).astype(bf16)
        for j in range(chunk):
            k = ch * chunk + j
            p = peer((2 * n - 2 - k) % n, x, z)
            block = served.at[ch, pl.ds(j * slots, slots)]

            def send():
                remote(block, fetched.at[me], f_s.at[p], f_r.at[me], dp, p).start()

            def keep():
                fetched[me] = served[ch, pl.ds(j * slots, slots)]

            if j == chunk - 1:
                pl.when(k < n - 1)(send)
                pl.when(k == n - 1)(keep)
            else:
                send()

    over(0, n // chunk, serve)
    over(mid, batch // 16, build)

    def line_to_partner(xo):
        xs = (x + xo) % NX

        def landed(zs):
            blk_ = hot.at[xs, zs, c]
            remote(blk_, blk_, xb_s.at[xo, zs], xb_r.at[xs, zs], dp, me).wait_recv()

        over(0, NZ, landed)
        line = hot.at[xs, :, c]
        remote(line, line, cc_s.at[xs], cc_r.at[xs], partner, me).start()

    over(1, NX, line_to_partner)

    for t in range(n):
        flat[:, pl.ds(t * slots, slots)] = asked[t][:, :slots]
    for b in range(rows // 128):
        sum_col[pl.ds(b * 128, 128), :] = to_column(eye(128, 128), sum_ref[pl.ds(b, 1), :])

    def finish_x(xs):
        line = hot.at[xs, :, 1 - c]
        remote(line, line, cc_s.at[xs], cc_r.at[xs], partner, me).wait_recv()

    over(0, NX, finish_x)
    acc[...] = jnp.dot(
        inc[:, pl.ds(0, hot_cols)], hot[...].reshape(hot_cols, width), preferred_element_type=f32
    )

    def fetched_wait(k):
        p = peer(k, x, z)
        remote(fetched.at[p], fetched.at[p], f_s.at[p], f_r.at[p], dp, p).wait_recv()

    over(0, n - 1, fetched_wait)
    slot_ids = lax.broadcasted_iota(i32, (slots, width), 0)

    def live(t):
        return slot_ids < count_ref[:, t : t + 1]

    for t in range(n):
        fetched[t] = jnp.where(live(t), fetched[t].astype(f32), 0.0).astype(bf16)
    pooled = (
        acc[...]
        + jnp.dot(
            inc[:, pl.ds(hot_cols, vocab - hot_cols)],
            fetched[...].reshape(n * slots, width),
            preferred_element_type=f32,
        )
    ).astype(bf16)

    load_w.wait()
    acc[...] = jnp.zeros_like(acc)
    hidden_units = w_v.shape[1]
    step = acc.shape[1]

    def forward(j):
        at = pl.ds(pl.multiple_of(j * step, step), step)
        pre_act = jnp.dot(pooled, w_v[:, at], preferred_element_type=f32)
        w = w_row[:, at]
        acc[...] += jnp.maximum(pre_act, 0.0).astype(bf16).astype(f32) * w
        wm[:, at] = jnp.where(pre_act > 0, w, 0.0).astype(bf16)

    over(0, hidden_units // step, forward, unroll=4)
    logit = jnp.sum(acc[...], axis=1, keepdims=True)
    lab = jnp.concatenate(
        [to_column(eye(128, 128), labels_ref[:, pl.ds(b * 128, 128)]) for b in range(batch // 128)], axis=0
    )
    dlogit = jax.nn.sigmoid(logit) - lab
    dpool[...] = jnp.zeros_like(dpool)
    deep = min(1024, hidden_units)

    def backward(j):
        at = pl.ds(pl.multiple_of(j * deep, deep), deep)
        dhidden = (dlogit * wm[:, at].astype(f32)).astype(bf16)
        dpool[...] += lax.dot_general(
            dhidden, w_v[:, at], (((1,), (1,)), ((), ())), preferred_element_type=f32
        )

    over(0, hidden_units // deep, backward)
    dpooled = dpool[...].astype(bf16)

    def slot_grad(at, size):
        return lax.dot_general(
            inc[:, pl.ds(at, size)], dpooled, (((0,), (0,)), ((), ())), preferred_element_type=f32
        )

    def core_copy(q):
        at = pl.ds(q * (n // parts), n // parts)
        return remote(hot_g.at[1 - c, at], hcore.at[at], hc_s.at[q], hc_r.at[q], partner, me)

    cold_step = min(256, n * slots)
    for k in range(n * slots // cold_step):
        g = slot_grad(hot_cols + k * cold_step, cold_step)
        for i in range(cold_step // slots):
            t = k * (cold_step // slots) + i
            cold_g[t] = jnp.where(live(t), g[i * slots : (i + 1) * slots], 0.0).astype(bf16)

    def cold_send(k):
        p = peer(k, x, z)
        to = ret.at[pl.ds(pl.multiple_of(me * slots, slots), slots)]
        remote(cold_g.at[p], to, c_s.at[p], c_r.at[me], dp, p).start()

    over(0, n - 1, cold_send)
    owners = 256 // hot_dev
    for k in range(hot_cols // 256):
        g = slot_grad(k * 256, 256).reshape(owners, NY, per_y, width).astype(bf16)
        for h in range(2):
            hot_g[h, pl.ds(k * owners, owners)] = g[..., h * 128 : (h + 1) * 128]
        done = (k + 1) * parts
        if done % (hot_cols // 256) == 0:
            core_copy(done // (hot_cols // 256) - 1).start()

    def y_copy(src, yt, q):
        at = pl.ds(q * (n // parts), n // parts)
        return remote(hsum.at[yt, at], hy.at[src, at], hy_s.at[yt, q], hy_r.at[src, q], dp_of(yt), me)

    for r in range(0, rows, 128):
        ids = lax.broadcasted_iota(i32, (128, n * slots), 0) + r
        oht[pl.ds(r, 128), :] = (ids == flat[...]).astype(f32).astype(bf16)
    for q in range(parts):
        core_copy(q).wait_recv()
        at = pl.ds(q * (n // parts), n // parts)

        def y_send(k):
            yt = y_peer(k, y)
            hsum[yt, at] = (hot_g[c, at, yt].astype(f32) + hcore[at, yt].astype(f32)).astype(bf16)

            @pl.when(k < NY - 1)
            def _():
                y_copy(y, yt, q).start()

        over(0, NY, y_send)
    ret[pl.ds(pl.multiple_of(me * slots, slots), slots), :] = cold_g[me]
    hsel[...] = (lax.broadcasted_iota(i32, (rows, 128), 0) == hot_pad[...]).astype(f32).astype(bf16)
    hfin[...] = jnp.zeros_like(hfin)

    def cold_wait(k):
        p = peer(k, x, z)
        to = ret.at[pl.ds(pl.multiple_of(p * slots, slots), slots)]
        remote(cold_g.at[p], to, c_s.at[p], c_r.at[p], dp, p).wait_recv()

    over(0, n - 1, cold_wait)

    pieces = 2
    per = subs // pieces
    piece_rows = rows // 2 // pieces

    def piece_grad(cc, i):
        at = pl.ds(pl.multiple_of(cc * (rows // 2) + i * piece_rows, piece_rows), piece_rows)
        g = jnp.dot(oht[at, :], ret[...], preferred_element_type=f32)
        gl[cc, pl.ds(i * per, per)] = g.astype(bf16).reshape(per, NY, sub, width)

    def g_core(b, yt):
        return remote(gl.at[1 - c, b, yt], gcore.at[b, yt], gc_s.at[b, yt], gc_r.at[b, yt], partner, me)

    def g_y(b, src, yt):
        return remote(gsum.at[b, yt], gy.at[b, src], gy_s.at[b, yt], gy_r.at[b, src], dp_of(yt), me)

    for i in range(pieces):
        piece_grad(1 - c, i)
        over(0, per * NY, lambda k: g_core(i * per + k // NY, y_peer(k % NY, y)).start())

    def g_send(k):
        b, yt = k // NY, y_peer(k % NY, y)
        g_core(b, yt).wait_recv()
        gsum[b, yt] = (gl[c, b, yt].astype(f32) + gcore[b, yt].astype(f32)).astype(bf16)

        @pl.when(k % NY < NY - 1)
        def _():
            g_y(b, y, yt).start()

    for i in range(pieces):
        piece_grad(c, i)
        over(i * per * NY, (i + 1) * per * NY, g_send)

    def y_wait(k):
        ys = (y + k) % NY
        for q in range(parts):
            y_copy(ys, ys, q).wait_recv()

    over(1, NY, y_wait)
    hy[y] = hsum[y]
    tot = hy[0].astype(f32)
    for k in range(1, NY):
        tot = tot + hy[k].astype(f32)
    hz[...] = tot.astype(bf16)

    def t_send(k):
        p = peer(k, x, z)
        remote(hz.at[p], ht.at[me], ht_s.at[p], ht_r.at[me], dp, p).start()

    over(0, n - 1, t_send)
    ht[me] = hz[me]

    def to_y(b, src, yt):
        part = total.at[c, b, src]
        return remote(part, part, ag_s.at[b, yt], ag_r.at[b, src], dp_of(yt), me)

    def to_core(cc, b, yt):
        part = total.at[cc, b, yt]
        return remote(part, part, ac_s.at[b, yt], ac_r.at[b, yt], partner, me)

    def dp_sum(b):
        over(1, NY, lambda k: g_y(b, (y + k) % NY, (y + k) % NY).wait_recv())
        gy[b, y] = gsum[b, y]
        tot = gy[b, 0].astype(f32)
        for k in range(1, NY):
            tot = tot + gy[b, k].astype(f32)
        total[c, b, y] = tot.astype(bf16)
        over(0, NY - 1, lambda k: to_y(b, y, y_peer(k, y)).start())
        to_core(c, b, y).start()

    over(0, subs, dp_sum)

    def t_wait(k):
        p = peer(k, x, z)
        remote(hz.at[p], ht.at[p], ht_s.at[p], ht_r.at[p], dp, p).wait_recv()

    over(0, n - 1, t_wait)
    hotf[c, pl.ds(pl.multiple_of(y * per_y, 8), per_y), :] = jnp.sum(ht[...].astype(f32), axis=0)

    def h_copy(src, to):
        b = hotf.at[src % 2, pl.ds(pl.multiple_of(src // 2 * per_y, 8), per_y)]
        return remote(b, b, ha_s.at[to], ha_r.at[src], to, me)

    over(1, 2 * NY, lambda k: h_copy(dp, (dp + k) % (2 * NY)).start())

    def h_wait(k):
        src = (dp + k) % (2 * NY)
        h_copy(src, src).wait_recv()

    def leave(cc, b):
        at = pl.ds(pl.multiple_of((cc * subs + b) * NY * sub, NY * sub), NY * sub)
        return pltpu.make_async_copy(new_rows.at[at], table_out.at[at], out_s.at[cc, b])

    def update(cc, b):
        tall = NY * sub
        at = pl.ds(pl.multiple_of((cc * subs + b) * tall, tall), tall)
        g = total[cc, b].astype(f32).reshape(tall, width) + gacc[at, :]
        new_sum = sum_col[at, :] + jnp.sum(g * g, axis=1, keepdims=True) * (1.0 / width)
        sum_col[at, :] = new_sum
        new_rows[at, :] = table_v[at, :] - g * (learning_rate / jnp.sqrt(new_sum))
        leave(cc, b).start()

    def gather(b):
        def landed(k):
            ys = (y + k) % NY
            to_y(b, ys, ys).wait_recv()
            to_core(c, b, ys).start()

        over(1, NY, landed)

    over(0, subs // 2, gather)
    over(1, 2 * NY, h_wait)
    for h in range(2):
        hfin[pl.ds(0, hot_dev), pl.ds(h * 128, 128)] = hotf[h]
    gacc[...] = jnp.dot(hsel[...], hfin[...].astype(bf16), preferred_element_type=f32)
    over(0, subs // 2, lambda b: update(c, b))

    def gather_update(b):
        gather(b)
        update(c, b)

    over(subs // 2, subs, gather_update)

    def gather_core(b):
        over(0, NY, lambda k: to_core(1 - c, b, k).wait_recv())
        update(1 - c, b)

    over(0, subs, gather_core)
    for b in range(rows // 128):
        sum_out[pl.ds(b, 1), :] = jnp.sum(
            jnp.where(eye(128, 128), sum_col[pl.ds(b * 128, 128), :], 0.0), axis=0, keepdims=True
        )

    for cc in range(2):
        over(0, subs, lambda b: leave(cc, b).wait())

    def finish_table(k):
        p = peer(k, x, z)
        remote(ids3.at[p], asked.at[me], ids_s.at[p], ids_r.at[me], dp, p).wait_send()
        remote(served.at[0, pl.ds(0, slots)], fetched.at[me], f_s.at[p], f_r.at[me], dp, p).wait_send()
        to = ret.at[pl.ds(pl.multiple_of(me * slots, slots), slots)]
        remote(cold_g.at[p], to, c_s.at[p], c_r.at[me], dp, p).wait_send()
        remote(hz.at[p], ht.at[me], ht_s.at[p], ht_r.at[me], dp, p).wait_send()

    over(0, n - 1, finish_table)

    def finish_hot(zo):
        blk_ = hot.at[x, z, c]

        @pl.when(zo > 0)
        def _():
            remote(blk_, blk_, za_s.at[zo], za_r.at[z], dp, me).wait_send()

        for xo in range(1, NX):
            remote(blk_, blk_, xb_s.at[xo, zo], xb_r.at[x, zo], dp, me).wait_send()

    over(0, NZ, finish_hot)

    def finish_line(xs):
        line = hot.at[xs, :, c]
        remote(line, line, cc_s.at[xs], cc_r.at[xs], partner, me).wait_send()

    over(0, NX, finish_line)
    for q in range(parts):
        core_copy(q).wait_send()

    def finish_y(k):
        yt = (y + k) % NY
        for q in range(parts):
            y_copy(y, yt, q).wait_send()

        def left(b):
            g_y(b, y, yt).wait_send()
            to_y(b, y, yt).wait_send()

        over(0, subs, left)

    over(1, NY, finish_y)
    over(1, 2 * NY, lambda k: h_copy(dp, (dp + k) % (2 * NY)).wait_send())

    def finish_core(k):
        g_core(k // NY, k % NY).wait_send()
        to_core(c, k // NY, k % NY).wait_send()

    over(0, subs * NY, finish_core)


def emit_kernel(table_ref, sum_ref, table_out, sum_out):
    table_out[...] = table_ref[...]
    sum_out[...] = sum_ref[...]


def per_device(bag_slots, labels, cold_ids, cold_count, table, adagrad_sum, hot_ids, w_in, w_out):
    n = NX * NZ
    batch, bag = bag_slots.shape
    rows, width = table.shape
    slots = cold_ids.shape[2]
    hot_dev = hot_ids.shape[0]
    hot_cols = n * hot_dev
    vocab = n * (hot_dev + slots)
    hidden = w_in.shape[1]
    chunk = min(8, n)
    per_y = hot_dev // NY
    parts = 2 if hot_cols % 512 == 0 else 1
    sub = 16
    subs = rows // (2 * NY * sub)
    groups = batch // 16
    dma = pltpu.SemaphoreType.DMA
    vmem = pl.BlockSpec(memory_space=pltpu.VMEM)
    hbm = pl.BlockSpec(memory_space=pl.ANY)
    new_table, new_sum = pl.pallas_call(
        functools.partial(step_kernel, groups // 4, groups // 2),
        name="step",
        out_shape=(
            jax.ShapeDtypeStruct((rows, width), f32),
            jax.ShapeDtypeStruct((rows // 128, 128), f32),
        ),
        in_specs=[hbm] * 9,
        out_specs=(hbm, vmem),
        scratch_shapes=[
            pltpu.VMEM((bag, batch), i32),
            pltpu.VMEM((1, batch), f32),
            pltpu.VMEM((n, slots), i32),
            pltpu.VMEM((1, n), i32),
            pltpu.VMEM((rows // 128, 128), f32),
            pltpu.VMEM((1, hot_dev), i32),
            pltpu.VMEM((hidden // 128, 128), bf16),
            pltpu.VMEM((rows, width), f32),
            pltpu.VMEM(w_in.shape, bf16),
            pltpu.VMEM((rows, width), bf16),
            pltpu.VMEM((n, 1, 128), i32),
            pltpu.VMEM((n, 1, 128), i32),
            pltpu.VMEM((1, n * slots), i32),
            pltpu.VMEM((1, 128), i32),
            pltpu.VMEM((batch, bag), i32),
            pltpu.VMEM((batch // 8, 8 * bag), i32),
            pltpu.VMEM((rows, 1), f32),
            pltpu.VMEM((NX, NZ, 2, hot_dev // 2, width), bf16),
            pltpu.VMEM((n, slots, width), bf16),
            pltpu.VMEM((chunk * slots, rows), bf16),
            pltpu.VMEM((n // chunk, chunk * slots, width), bf16),
            pltpu.VMEM((batch, vocab), bf16),
            pltpu.VMEM((batch, hidden), bf16),
            pltpu.VMEM((batch, 256), f32),
            pltpu.VMEM((batch, width), f32),
            pltpu.VMEM((2, n, NY, per_y, 128), bf16),
            pltpu.VMEM((n, slots, width), bf16),
            pltpu.VMEM((n, NY, per_y, 128), bf16),
            pltpu.VMEM((NY, n, per_y, 128), bf16),
            pltpu.VMEM((NY, n, per_y, 128), bf16),
            pltpu.VMEM((n, per_y, 128), bf16),
            pltpu.VMEM((n, per_y, 128), bf16),
            pltpu.VMEM((n * slots, width), bf16),
            pltpu.VMEM((rows, n * slots), bf16),
            pltpu.VMEM((rows, width), f32),
            pltpu.VMEM((128, width), f32),
            pltpu.VMEM((rows, 128), bf16),
            pltpu.VMEM((2, hot_dev, 128), f32),
            pltpu.VMEM((1, hidden), f32),
            pltpu.VMEM((2, subs, NY, sub, width), bf16),
            pltpu.VMEM((subs, NY, sub, width), bf16),
            pltpu.VMEM((subs, NY, sub, width), bf16),
            pltpu.VMEM((subs, NY, sub, width), bf16),
            pltpu.VMEM((2, subs, NY, sub, width), bf16),
            pltpu.VMEM((rows, width), f32),
            dma((9,)),
            dma((2, subs)),
            dma((n,)), dma((n,)),
            dma((NZ,)), dma((NZ,)),
            dma((NX, NZ)), dma((NX, NZ)),
            dma((NX,)), dma((NX,)),
            dma((n,)), dma((n,)),
            dma((parts,)), dma((parts,)),
            dma((NY, parts)), dma((NY, parts)),
            dma((n,)), dma((n,)),
            dma((n,)), dma((n,)),
            dma((subs, NY)), dma((subs, NY)),
            dma((subs, NY)), dma((subs, NY)),
            dma((subs, NY)), dma((subs, NY)),
            dma((subs, NY)), dma((subs, NY)),
            dma((2 * NY,)), dma((2 * NY,)),
        ],
        compiler_params=pltpu.CompilerParams(
            collective_id=0, has_side_effects=True, vmem_limit_bytes=60 << 20
        ),
    )(
        table,
        w_in,
        bag_slots.T,
        labels.reshape(1, batch),
        cold_ids[0],
        cold_count,
        adagrad_sum.reshape(rows // 128, 128),
        hot_ids.reshape(1, hot_dev),
        w_out.reshape(hidden // 128, 128),
    )
    part = pl.BlockSpec((rows // 4, width), lambda i: (i, 0))
    whole = pl.BlockSpec((rows // 128, 128), lambda i: (0, 0))
    out_table, out_sum = pl.pallas_call(
        emit_kernel,
        name="emit",
        out_shape=(
            jax.ShapeDtypeStruct((rows, width), f32),
            jax.ShapeDtypeStruct((rows // 128, 128), f32),
        ),
        grid=(4,),
        in_specs=[part, whole],
        out_specs=(part, whole),
    )(new_table, new_sum)
    return out_table, out_sum.reshape(rows)


def solution(mesh):
    placed = (
        P(("dp", "table"), None),
        P(("dp", "table")),
        P(("dp", "table"), None, None),
        P(("dp", "table"), None),
        P("table", None),
        P("table"),
        P("table"),
        P(),
        P(),
    )
    return jax.shard_map(
        per_device,
        mesh=mesh,
        in_specs=placed,
        out_specs=(P("table", None), P("table")),
        check_vma=False,
    )
```

```python
import functools

import jax
import jax.numpy as jnp
from jax import lax
from jax.experimental import pallas as pl
from jax.experimental.pallas import tpu as pltpu
from jax.sharding import PartitionSpec as P

MESH = pl.DeviceIdType.MESH
learning_rate = 0.3
NX, NZ, NY = 4, 8, 8
bf16, f32, i32 = jnp.bfloat16, jnp.float32, jnp.int32


def remote(src, dst, send_sem, recv_sem, dp, table):
    return pltpu.make_async_remote_copy(
        src_ref=src,
        dst_ref=dst,
        send_sem=send_sem,
        recv_sem=recv_sem,
        device_id=(dp, table),
        device_id_type=MESH,
    )


def ring(a, size):
    return lax.rem(a, size)


def peer(k, x, z):
    m = lax.div(k, NX)
    kz = NZ + NZ // 2 + (1 - 2 * lax.rem(m, 2)) * lax.div(m + 1, 2)
    return ring(x + k + 1, NX) * NZ + ring(z + kz, NZ)


def y_peer(k, y):
    return ring(y + NY + NY // 2 + (1 - 2 * lax.rem(k, 2)) * lax.div(k + 1, 2), NY)


def place():
    dp, me = lax.axis_index("dp"), lax.axis_index("table")
    y, c = lax.div(dp, 2), lax.rem(dp, 2)
    x, z = lax.div(me, NZ), lax.rem(me, NZ)
    partner = y * 2 + (1 - c)
    return dp, me, y, c, x, z, partner


def step_kernel(
    pre, mid,
    table_hbm, w_hbm, bag_hbm, labels_hbm, ids_hbm, count_hbm, sum_hbm, hot_ids_hbm, w_out_hbm,
    table_out, sum_out,
    bag_ref, labels_ref, ids_ref, count_ref, sum_ref, hot_ids_ref, w_out_ref,
    table_v, w_v, tb, ids3, asked, flat, hot_pad, bag_rows, bag2, sum_col,
    hot, fetched, oh, served, inc, wm, acc, dpool,
    hot_g, cold_g, hcore, hsum, hy, hz, ht, ret, oht, gacc, hfin, hsel, hotf, w_row, live, gl, gcore, gsum, gy, total,
    in_s, ids_s, ids_r, za_s, za_r, xb_s, xb_r, cc_s, cc_r, f_s, f_r,
    hc_s, hc_r, hy_s, hy_r, ht_s, ht_r, c_s, c_r, gc_s, gc_r, gy_s, gy_r, ag_s, ag_r, ac_s, ac_r, ha_s, ha_r,
):
    n = NX * NZ
    dp, me, y, c, x, z, partner = place()
    rows, width = table_v.shape
    slots = fetched.shape[1]
    half = hot.shape[3]
    hot_dev = 2 * half
    hot_cols = n * hot_dev
    per_y = hz.shape[1]
    batch, vocab = inc.shape
    parts = hc_s.shape[0]
    subs, sub = gl.shape[1], gl.shape[3]

    def dp_of(yy):
        return yy * 2 + c

    def over(lo, hi, body, unroll=1):
        def run(k, _):
            body(k)
            return 0

        lax.fori_loop(lo, hi, run, 0, unroll=unroll)

    def other(k):
        return ring(me + 1 + k, n)

    def eye(a, b, shift=0):
        return lax.broadcasted_iota(i32, (a, b), 0) + shift == lax.broadcasted_iota(i32, (a, b), 1)

    def to_column(mask, row):
        return jnp.sum(jnp.where(mask, row, 0.0), axis=1, keepdims=True)

    barrier = pltpu.get_barrier_semaphore()
    over(0, n - 1, lambda k: pl.semaphore_signal(
        barrier, inc=1, device_id=(dp, peer(k, x, z)), device_id_type=MESH))
    over(1, 2 * NY, lambda k: pl.semaphore_signal(
        barrier, inc=1, device_id=(ring(dp + k, 2 * NY), me), device_id_type=MESH))

    small = (
        (ids_hbm, ids_ref), (hot_ids_hbm, hot_ids_ref), (bag_hbm, bag_ref), (w_out_hbm, w_out_ref),
        (count_hbm, count_ref), (sum_hbm, sum_ref), (labels_hbm, labels_ref),
    )
    loads = [pltpu.make_async_copy(a, b, in_s.at[i + 2]) for i, (a, b) in enumerate(small)]
    load_table = pltpu.make_async_copy(table_hbm, table_v, in_s.at[0])
    load_w = pltpu.make_async_copy(w_hbm, w_v, in_s.at[1])
    for load in loads[:2]:
        load.start()
    load_table.start()
    for load in loads[2:]:
        load.start()
    load_w.start()
    for load in loads:
        load.wait()

    ids3[...] = jnp.full_like(ids3, -1)
    for t in range(n):
        ids3[t, :, pl.ds(0, slots)] = ids_ref[pl.ds(t, 1), :]
    hot_pad[...] = jnp.full_like(hot_pad, -1)
    hot_pad[:, pl.ds(0, hot_dev)] = hot_ids_ref[...]
    for k in range(w_out_ref.shape[0]):
        w_row[:, pl.ds(k * 128, 128)] = w_out_ref[pl.ds(k, 1), :].astype(f32)
    lane = lax.broadcasted_iota(i32, (1, slots), 1)
    for t in range(n):
        live[:, pl.ds(t * slots, slots)] = (lane < count_ref[:, t : t + 1]).astype(f32)
    bag = bag_ref.shape[0]
    bag_rows[...] = bag_ref[...].T
    for s in range(8):
        bag2[:, pl.ds(s * bag, bag)] = bag_rows[pl.ds(s, batch // 8, stride=8), :]

    entries = 8 * bag
    tiles = vocab // 128
    own = lax.broadcasted_iota(i32, (8, entries), 1) // bag == lax.broadcasted_iota(i32, (8, entries), 0)
    tile_ids = lax.broadcasted_iota(i32, (tiles, 8, entries), 0)
    lane_ids = lax.broadcasted_iota(i32, (128, entries), 0)

    def build(i):
        outs = []
        for h in range(2):
            v = bag2[pl.ds(2 * i + h, 1), :]
            key = jnp.where(own, v >> 7, -1)
            left = (key[None] == tile_ids).astype(f32).reshape(tiles * 8, entries).astype(bf16)
            right = (lane_ids == (v & 127)).astype(f32).astype(bf16)
            outs.append(
                lax.dot_general(left, right, (((1,), (1,)), ((), ())), preferred_element_type=f32)
            )
        at = pl.ds(pl.multiple_of(16 * i, 16), 16)
        for k in range(tiles):
            t = jnp.concatenate([outs[0][8 * k : 8 * k + 8], outs[1][8 * k : 8 * k + 8]], axis=0)
            if k * 128 >= hot_cols:
                t = t * live[:, pl.ds(k * 128 - hot_cols, 128)]
            inc[at, pl.ds(k * 128, 128)] = t.astype(bf16)

    load_table.wait()
    tb[...] = table_v[...].astype(bf16)
    hot_col = to_column(eye(half, 128, c * half), hot_pad[...].astype(f32))
    hot_sel = (hot_col == lax.broadcasted_iota(i32, (half, rows), 1).astype(f32)).astype(f32).astype(bf16)
    hot[x, z, c] = jnp.dot(hot_sel, tb[...], preferred_element_type=f32).astype(bf16)
    asked[me] = ids3[me]
    over(0, pre, build)
    pl.semaphore_wait(barrier, n - 1 + 2 * NY - 1)

    def send_ids(k):
        p = peer(k, x, z)
        remote(ids3.at[p], asked.at[me], ids_s.at[p], ids_r.at[me], dp, p).start()

    over(0, n - 1, send_ids)

    def hot_to_x(zs, xo):
        blk_ = hot.at[x, zs, c]
        remote(blk_, blk_, xb_s.at[xo, zs], xb_r.at[x, zs], dp, (ring(x + xo, NX)) * NZ + z).start()

    def hot_to_z(zo):
        blk_ = hot.at[x, z, c]
        remote(blk_, blk_, za_s.at[zo], za_r.at[z], dp, x * NZ + ring(z + zo, NZ)).start()

    over(1, NZ, hot_to_z)
    for xo in range(1, NX):
        hot_to_x(z, xo)
    over(pre, mid, build)

    def forward_x(zo):
        zs = ring(z + zo, NZ)
        blk_ = hot.at[x, zs, c]
        remote(blk_, blk_, za_s.at[zo], za_r.at[zs], dp, me).wait_recv()
        for xo in range(1, NX):
            hot_to_x(zs, xo)

    over(1, NZ, forward_x)
    line = hot.at[x, :, c]
    remote(line, line, cc_s.at[x], cc_r.at[x], partner, me).start()

    request = eye(slots, 128)
    chunk = served.shape[1] // slots

    def serve(ch):
        for j in range(chunk):
            k = ch * chunk + j
            p = peer(ring(2 * n - 2 - k, n), x, z)

            def arrived():
                remote(ids3.at[p], asked.at[p], ids_s.at[p], ids_r.at[p], dp, p).wait_recv()

            if j == chunk - 1:
                pl.when(k < n - 1)(arrived)
            else:
                arrived()
            col = to_column(request, asked[p].astype(f32))
            hit = col == lax.broadcasted_iota(i32, (slots, rows), 1).astype(f32)
            oh[pl.ds(j * slots, slots), :] = hit.astype(f32).astype(bf16)
        served[ch] = jnp.dot(oh[...], tb[...], preferred_element_type=f32).astype(bf16)
        for j in range(chunk):
            k = ch * chunk + j
            p = peer(ring(2 * n - 2 - k, n), x, z)
            block = served.at[ch, pl.ds(j * slots, slots)]

            def send():
                remote(block, fetched.at[me], f_s.at[p], f_r.at[me], dp, p).start()

            def keep():
                fetched[me] = served[ch, pl.ds(j * slots, slots)]

            if j == chunk - 1:
                pl.when(k < n - 1)(send)
                pl.when(k == n - 1)(keep)
            else:
                send()

    over(0, n // chunk, serve)
    over(mid, batch // 16, build)

    def line_to_partner(xo):
        xs = ring(x + xo, NX)

        def landed(zs):
            blk_ = hot.at[xs, zs, c]
            remote(blk_, blk_, xb_s.at[xo, zs], xb_r.at[xs, zs], dp, me).wait_recv()

        over(0, NZ, landed)
        line = hot.at[xs, :, c]
        remote(line, line, cc_s.at[xs], cc_r.at[xs], partner, me).start()

    over(1, NX, line_to_partner)

    for t in range(n):
        flat[:, pl.ds(t * slots, slots)] = asked[t][:, :slots]
    for b in range(rows // 128):
        sum_col[pl.ds(b * 128, 128), :] = to_column(eye(128, 128), sum_ref[pl.ds(b, 1), :])

    def finish_x(xs):
        line = hot.at[xs, :, 1 - c]
        remote(line, line, cc_s.at[xs], cc_r.at[xs], partner, me).wait_recv()

    over(0, NX, finish_x)
    acc[...] = jnp.dot(
        inc[:, pl.ds(0, hot_cols)], hot[...].reshape(hot_cols, width), preferred_element_type=f32
    )

    def fetched_wait(k):
        p = other(k)
        remote(fetched.at[p], fetched.at[p], f_s.at[p], f_r.at[p], dp, p).wait_recv()

    over(0, n - 1, fetched_wait)
    pooled = (
        acc[...]
        + jnp.dot(
            inc[:, pl.ds(hot_cols, vocab - hot_cols)],
            fetched[...].reshape(n * slots, width),
            preferred_element_type=f32,
        )
    ).astype(bf16)

    load_w.wait()
    acc[...] = jnp.zeros_like(acc)
    hidden_units = w_v.shape[1]
    step = acc.shape[1]

    def forward(j):
        at = pl.ds(pl.multiple_of(j * step, step), step)
        pre_act = jnp.dot(pooled, w_v[:, at], preferred_element_type=f32)
        w = w_row[:, at]
        acc[...] += jnp.maximum(pre_act, 0.0).astype(bf16).astype(f32) * w
        wm[:, at] = jnp.where(pre_act > 0, w, 0.0).astype(bf16)

    over(0, hidden_units // step, forward, unroll=4)
    logit = jnp.sum(acc[...], axis=1, keepdims=True)
    lab = jnp.concatenate(
        [to_column(eye(128, 128), labels_ref[:, pl.ds(b * 128, 128)]) for b in range(batch // 128)], axis=0
    )
    dlogit = jax.nn.sigmoid(logit) - lab
    dpool[...] = jnp.zeros_like(dpool)
    deep = min(1024, hidden_units)

    def backward(j):
        at = pl.ds(pl.multiple_of(j * deep, deep), deep)
        dhidden = (dlogit * wm[:, at].astype(f32)).astype(bf16)
        dpool[...] += lax.dot_general(
            dhidden, w_v[:, at], (((1,), (1,)), ((), ())), preferred_element_type=f32
        )

    over(0, hidden_units // deep, backward)
    dpooled = dpool[...].astype(bf16)

    def slot_grad(at, size):
        return lax.dot_general(
            inc[:, pl.ds(at, size)], dpooled, (((0,), (0,)), ((), ())), preferred_element_type=f32
        )

    def core_copy(q):
        at = pl.ds(q * (n // parts), n // parts)
        return remote(hot_g.at[1 - c, at], hcore.at[at], hc_s.at[q], hc_r.at[q], partner, me)

    cold_step = min(256, n * slots)
    for k in range(n * slots // cold_step):
        g = slot_grad(hot_cols + k * cold_step, cold_step)
        for i in range(cold_step // slots):
            t = k * (cold_step // slots) + i
            cold_g[t] = g[i * slots : (i + 1) * slots].astype(bf16)

    def cold_send(k):
        p = peer(k, x, z)
        to = ret.at[pl.ds(pl.multiple_of(me * slots, slots), slots)]
        remote(cold_g.at[p], to, c_s.at[p], c_r.at[me], dp, p).start()

    over(0, n - 1, cold_send)
    owners = 256 // hot_dev
    for k in range(hot_cols // 256):
        g = slot_grad(k * 256, 256).reshape(owners, NY, per_y, width).astype(bf16)
        for h in range(2):
            hot_g[h, pl.ds(k * owners, owners)] = g[..., h * 128 : (h + 1) * 128]
        done = (k + 1) * parts
        if done % (hot_cols // 256) == 0:
            core_copy(done // (hot_cols // 256) - 1).start()

    def y_copy(src, yt, q):
        at = pl.ds(q * (n // parts), n // parts)
        return remote(hsum.at[yt, at], hy.at[src, at], hy_s.at[yt, q], hy_r.at[src, q], dp_of(yt), me)

    for r in range(0, rows, 128):
        ids = lax.broadcasted_iota(i32, (128, n * slots), 0) + r
        oht[pl.ds(r, 128), :] = (ids == flat[...]).astype(f32).astype(bf16)
    for q in range(parts):
        core_copy(q).wait_recv()
        at = pl.ds(q * (n // parts), n // parts)

        def y_send(k):
            yt = y_peer(k, y)
            hsum[yt, at] = (hot_g[c, at, yt].astype(f32) + hcore[at, yt].astype(f32)).astype(bf16)

            @pl.when(k < NY - 1)
            def _():
                y_copy(y, yt, q).start()

        over(0, NY, y_send)
    ret[pl.ds(pl.multiple_of(me * slots, slots), slots), :] = cold_g[me]
    hsel[...] = (lax.broadcasted_iota(i32, (rows, 128), 0) == hot_pad[...]).astype(f32).astype(bf16)
    hfin[...] = jnp.zeros_like(hfin)

    def finish_fetch(k):
        p = other(k)
        remote(ids3.at[p], asked.at[me], ids_s.at[p], ids_r.at[me], dp, p).wait_send()
        remote(served.at[0, pl.ds(0, slots)], fetched.at[me], f_s.at[p], f_r.at[me], dp, p).wait_send()

    over(0, n - 1, finish_fetch)

    def finish_hot(zo):
        blk_ = hot.at[x, z, c]

        @pl.when(zo > 0)
        def _():
            remote(blk_, blk_, za_s.at[zo], za_r.at[z], dp, me).wait_send()

        for xo in range(1, NX):
            remote(blk_, blk_, xb_s.at[xo, zo], xb_r.at[x, zo], dp, me).wait_send()

    over(0, NZ, finish_hot)

    def finish_line(xs):
        line = hot.at[xs, :, c]
        remote(line, line, cc_s.at[xs], cc_r.at[xs], partner, me).wait_send()

    over(0, NX, finish_line)
    def cold_wait(k):
        p = other(k)
        to = ret.at[pl.ds(pl.multiple_of(p * slots, slots), slots)]
        remote(cold_g.at[p], to, c_s.at[p], c_r.at[p], dp, p).wait_recv()

    over(0, n - 1, cold_wait)

    pieces = 2
    per = subs // pieces
    piece_rows = rows // 2 // pieces

    def piece_grad(cc, i):
        at = pl.ds(pl.multiple_of(cc * (rows // 2) + i * piece_rows, piece_rows), piece_rows)
        g = jnp.dot(oht[at, :], ret[...], preferred_element_type=f32)
        gl[cc, pl.ds(i * per, per)] = g.astype(bf16).reshape(per, NY, sub, width)

    def g_core(b, yt):
        return remote(gl.at[1 - c, b, yt], gcore.at[b, yt], gc_s.at[b, yt], gc_r.at[b, yt], partner, me)

    def g_y(b, src, yt):
        return remote(gsum.at[b, yt], gy.at[b, src], gy_s.at[b, yt], gy_r.at[b, src], dp_of(yt), me)

    for i in range(pieces):
        piece_grad(1 - c, i)
        over(0, per * NY, lambda k: g_core(i * per + lax.div(k, NY), y_peer(ring(k, NY), y)).start())

    def g_send(k):
        b, yt = lax.div(k, NY), y_peer(ring(k, NY), y)
        g_core(b, yt).wait_recv()
        gsum[b, yt] = (gl[c, b, yt].astype(f32) + gcore[b, yt].astype(f32)).astype(bf16)

        @pl.when(ring(k, NY) < NY - 1)
        def _():
            g_y(b, y, yt).start()

    for i in range(pieces):
        piece_grad(c, i)
        over(i * per * NY, (i + 1) * per * NY, g_send)

    def y_wait(k):
        ys = ring(y + k, NY)
        for q in range(parts):
            y_copy(ys, ys, q).wait_recv()

    over(1, NY, y_wait)
    hy[y] = hsum[y]
    tot = hy[0].astype(f32)
    for k in range(1, NY):
        tot = tot + hy[k].astype(f32)
    hz[...] = tot.astype(bf16)

    def t_send(k):
        p = peer(k, x, z)
        remote(hz.at[p], ht.at[me], ht_s.at[p], ht_r.at[me], dp, p).start()

    over(0, n - 1, t_send)
    ht[me] = hz[me]

    def to_y(b, src, yt):
        part = total.at[c, b, src]
        return remote(part, part, ag_s.at[b, yt], ag_r.at[b, src], dp_of(yt), me)

    def to_core(cc, b, yt):
        part = total.at[cc, b, yt]
        return remote(part, part, ac_s.at[b, yt], ac_r.at[b, yt], partner, me)

    def dp_sum(b):
        over(1, NY, lambda k: g_y(b, ring(y + k, NY), ring(y + k, NY)).wait_recv())
        gy[b, y] = gsum[b, y]
        tot = gy[b, 0].astype(f32)
        for k in range(1, NY):
            tot = tot + gy[b, k].astype(f32)
        total[c, b, y] = tot.astype(bf16)
        over(0, NY - 1, lambda k: to_y(b, y, y_peer(k, y)).start())
        to_core(c, b, y).start()

    over(0, subs, dp_sum)

    def t_wait(k):
        p = other(k)
        remote(hz.at[p], ht.at[p], ht_s.at[p], ht_r.at[p], dp, p).wait_recv()

    over(0, n - 1, t_wait)
    hotf[c, pl.ds(pl.multiple_of(y * per_y, 8), per_y), :] = jnp.sum(ht[...].astype(f32), axis=0)

    def h_copy(src, to):
        b = hotf.at[lax.rem(src, 2), pl.ds(pl.multiple_of(lax.div(src, 2) * per_y, 8), per_y)]
        return remote(b, b, ha_s.at[to], ha_r.at[src], to, me)

    over(1, 2 * NY, lambda k: h_copy(dp, ring(dp + k, 2 * NY)).start())

    def h_wait(k):
        src = ring(dp + k, 2 * NY)
        h_copy(src, src).wait_recv()

    def update(cc, b):
        tall = NY * sub
        at = pl.ds(pl.multiple_of((cc * subs + b) * tall, tall), tall)
        g = total[cc, b].astype(f32).reshape(tall, width) + gacc[at, :]
        new_sum = sum_col[at, :] + jnp.sum(g * g, axis=1, keepdims=True) * (1.0 / width)
        sum_col[at, :] = new_sum
        table_out[at, :] = table_v[at, :] - g * (learning_rate / jnp.sqrt(new_sum))

    def gather(b):
        def landed(k):
            ys = ring(y + k, NY)
            to_y(b, ys, ys).wait_recv()
            to_core(c, b, ys).start()

        over(1, NY, landed)

    def finish_table(k):
        p = other(k)
        to = ret.at[pl.ds(pl.multiple_of(me * slots, slots), slots)]
        remote(cold_g.at[p], to, c_s.at[p], c_r.at[me], dp, p).wait_send()
        remote(hz.at[p], ht.at[me], ht_s.at[p], ht_r.at[me], dp, p).wait_send()

    def finish_sums(k):
        yt = ring(y + k, NY)
        for q in range(parts):
            y_copy(y, yt, q).wait_send()
        over(0, subs, lambda b: g_y(b, y, yt).wait_send())

    over(0, subs // 2, gather)
    over(0, n - 1, finish_table)
    over(1, NY, finish_sums)
    for q in range(parts):
        core_copy(q).wait_send()
    over(0, subs * NY, lambda k: g_core(lax.div(k, NY), ring(k, NY)).wait_send())
    over(1, 2 * NY, h_wait)
    for h in range(2):
        hfin[pl.ds(0, hot_dev), pl.ds(h * 128, 128)] = hotf[h]
    gacc[...] = jnp.dot(hsel[...], hfin[...].astype(bf16), preferred_element_type=f32)
    over(0, subs // 2, lambda b: update(c, b))

    def gather_update(b):
        gather(b)
        update(c, b)

    over(subs // 2, subs, gather_update)

    def gather_core(b):
        over(0, NY, lambda k: to_core(1 - c, b, k).wait_recv())
        update(1 - c, b)

    over(0, subs, gather_core)
    for b in range(rows // 128):
        sum_out[pl.ds(b, 1), :] = jnp.sum(
            jnp.where(eye(128, 128), sum_col[pl.ds(b * 128, 128), :], 0.0), axis=0, keepdims=True
        )

    def finish_y(k):
        yt = ring(y + k, NY)
        over(0, subs, lambda b: to_y(b, y, yt).wait_send())

    over(1, NY, finish_y)
    over(0, subs * NY, lambda k: to_core(c, lax.div(k, NY), ring(k, NY)).wait_send())
    over(1, 2 * NY, lambda k: h_copy(dp, ring(dp + k, 2 * NY)).wait_send())


def emit_kernel(table_ref, sum_ref, table_out, sum_out, sems):
    copies = [
        pltpu.make_async_copy(table_ref, table_out, sems.at[0]),
        pltpu.make_async_copy(sum_ref, sum_out, sems.at[1]),
    ]
    for copy in copies:
        copy.start()
    for copy in copies:
        copy.wait()


def per_device(bag_slots, labels, cold_ids, cold_count, table, adagrad_sum, hot_ids, w_in, w_out):
    n = NX * NZ
    batch, bag = bag_slots.shape
    rows, width = table.shape
    slots = cold_ids.shape[2]
    hot_dev = hot_ids.shape[0]
    hot_cols = n * hot_dev
    vocab = n * (hot_dev + slots)
    hidden = w_in.shape[1]
    chunk = min(8, n)
    per_y = hot_dev // NY
    parts = 2 if hot_cols % 512 == 0 else 1
    sub = 16
    subs = rows // (2 * NY * sub)
    groups = batch // 16
    dma = pltpu.SemaphoreType.DMA
    vmem = pl.BlockSpec(memory_space=pltpu.VMEM)
    hbm = pl.BlockSpec(memory_space=pltpu.HBM)
    new_table, new_sum = pl.pallas_call(
        functools.partial(step_kernel, groups // 4, groups // 2),
        name="step",
        out_shape=(
            jax.ShapeDtypeStruct((rows, width), f32),
            jax.ShapeDtypeStruct((rows // 128, 128), f32),
        ),
        in_specs=[hbm] * 9,
        out_specs=(vmem, vmem),
        scratch_shapes=[
            pltpu.VMEM((bag, batch), i32),
            pltpu.VMEM((1, batch), f32),
            pltpu.VMEM((n, slots), i32),
            pltpu.VMEM((1, n), i32),
            pltpu.VMEM((rows // 128, 128), f32),
            pltpu.VMEM((1, hot_dev), i32),
            pltpu.VMEM((hidden // 128, 128), bf16),
            pltpu.VMEM((rows, width), f32),
            pltpu.VMEM(w_in.shape, bf16),
            pltpu.VMEM((rows, width), bf16),
            pltpu.VMEM((n, 1, 128), i32),
            pltpu.VMEM((n, 1, 128), i32),
            pltpu.VMEM((1, n * slots), i32),
            pltpu.VMEM((1, 128), i32),
            pltpu.VMEM((batch, bag), i32),
            pltpu.VMEM((batch // 8, 8 * bag), i32),
            pltpu.VMEM((rows, 1), f32),
            pltpu.VMEM((NX, NZ, 2, hot_dev // 2, width), bf16),
            pltpu.VMEM((n, slots, width), bf16),
            pltpu.VMEM((chunk * slots, rows), bf16),
            pltpu.VMEM((n // chunk, chunk * slots, width), bf16),
            pltpu.VMEM((batch, vocab), bf16),
            pltpu.VMEM((batch, hidden), bf16),
            pltpu.VMEM((batch, 256), f32),
            pltpu.VMEM((batch, width), f32),
            pltpu.VMEM((2, n, NY, per_y, 128), bf16),
            pltpu.VMEM((n, slots, width), bf16),
            pltpu.VMEM((n, NY, per_y, 128), bf16),
            pltpu.VMEM((NY, n, per_y, 128), bf16),
            pltpu.VMEM((NY, n, per_y, 128), bf16),
            pltpu.VMEM((n, per_y, 128), bf16),
            pltpu.VMEM((n, per_y, 128), bf16),
            pltpu.VMEM((n * slots, width), bf16),
            pltpu.VMEM((rows, n * slots), bf16),
            pltpu.VMEM((rows, width), f32),
            pltpu.VMEM((128, width), f32),
            pltpu.VMEM((rows, 128), bf16),
            pltpu.VMEM((2, hot_dev, 128), f32),
            pltpu.VMEM((1, hidden), f32),
            pltpu.VMEM((1, n * slots), f32),
            pltpu.VMEM((2, subs, NY, sub, width), bf16),
            pltpu.VMEM((subs, NY, sub, width), bf16),
            pltpu.VMEM((subs, NY, sub, width), bf16),
            pltpu.VMEM((subs, NY, sub, width), bf16),
            pltpu.VMEM((2, subs, NY, sub, width), bf16),
            dma((9,)),
            dma((n,)), dma((n,)),
            dma((NZ,)), dma((NZ,)),
            dma((NX, NZ)), dma((NX, NZ)),
            dma((NX,)), dma((NX,)),
            dma((n,)), dma((n,)),
            dma((parts,)), dma((parts,)),
            dma((NY, parts)), dma((NY, parts)),
            dma((n,)), dma((n,)),
            dma((n,)), dma((n,)),
            dma((subs, NY)), dma((subs, NY)),
            dma((subs, NY)), dma((subs, NY)),
            dma((subs, NY)), dma((subs, NY)),
            dma((subs, NY)), dma((subs, NY)),
            dma((2 * NY,)), dma((2 * NY,)),
        ],
        compiler_params=pltpu.CompilerParams(
            collective_id=0, has_side_effects=True, vmem_limit_bytes=44 << 20
        ),
    )(*[pltpu.with_memory_space_constraint(v, pltpu.HBM) for v in (
        table,
        w_in,
        bag_slots.T,
        labels.reshape(1, batch),
        cold_ids[0],
        cold_count,
        adagrad_sum.reshape(rows // 128, 128),
        hot_ids.reshape(1, hot_dev),
        w_out.reshape(hidden // 128, 128),
    )])
    out_table, out_sum = pl.pallas_call(
        emit_kernel,
        name="emit",
        out_shape=(
            jax.ShapeDtypeStruct((rows, width), f32),
            jax.ShapeDtypeStruct((rows // 128, 128), f32),
        ),
        in_specs=[vmem, vmem],
        out_specs=(hbm, hbm),
        scratch_shapes=[dma((2,))],
        compiler_params=pltpu.CompilerParams(vmem_limit_bytes=4 << 20),
    )(new_table, new_sum)
    return out_table, out_sum.reshape(rows)


def solution(mesh):
    placed = (
        P(("dp", "table"), None),
        P(("dp", "table")),
        P(("dp", "table"), None, None),
        P(("dp", "table"), None),
        P("table", None),
        P("table"),
        P("table"),
        P(),
        P(),
    )
    return jax.shard_map(
        per_device,
        mesh=mesh,
        in_specs=placed,
        out_specs=(P("table", None), P("table")),
        check_vma=False,
    )
```

```python
import functools

import jax
import jax.numpy as jnp
from jax import lax
from jax.experimental import pallas as pl
from jax.experimental.pallas import tpu as pltpu
from jax.sharding import PartitionSpec as P

MESH = pl.DeviceIdType.MESH
learning_rate = 0.3
NX, NZ, NY = 4, 8, 8
bf16, f32, i32 = jnp.bfloat16, jnp.float32, jnp.int32


def remote(src, dst, send_sem, recv_sem, dp, table):
    return pltpu.make_async_remote_copy(
        src_ref=src,
        dst_ref=dst,
        send_sem=send_sem,
        recv_sem=recv_sem,
        device_id=(dp, table),
        device_id_type=MESH,
    )


def ring(a, size):
    return lax.rem(a, size)


def peer(k, x, z):
    m = lax.div(k, NX)
    kz = NZ + NZ // 2 + (1 - 2 * lax.rem(m, 2)) * lax.div(m + 1, 2)
    return ring(x + k + 1, NX) * NZ + ring(z + kz, NZ)


def y_peer(k, y):
    return ring(y + NY + NY // 2 + (1 - 2 * lax.rem(k, 2)) * lax.div(k + 1, 2), NY)


def place():
    dp, me = lax.axis_index("dp"), lax.axis_index("table")
    y, c = lax.div(dp, 2), lax.rem(dp, 2)
    x, z = lax.div(me, NZ), lax.rem(me, NZ)
    partner = y * 2 + (1 - c)
    return dp, me, y, c, x, z, partner


def step_kernel(
    pre, mid,
    table_hbm, w_hbm, bag_hbm, labels_hbm, ids_hbm, count_hbm, sum_hbm, hot_ids_hbm, w_out_hbm,
    table_out, sum_out,
    bag_ref, labels_ref, ids_ref, count_ref, sum_ref, hot_ids_ref, w_out_ref,
    table_v, w_v, tb, ids3, asked, flat, hot_pad, bag_rows, bag2, sum_col,
    hot, fetched, oh, served, inc, wm, acc, dpool,
    hot_g, cold_g, hcore, hsum, hy, hz, ht, ret, oht, gacc, hfin, hsel, hotf, w_row, live, gl, gcore, gsum, gy, total,
    in_s, ids_s, ids_r, za_s, za_r, xb_s, xb_r, cc_s, cc_r, f_s, f_r,
    hc_s, hc_r, hy_s, hy_r, ht_s, ht_r, c_s, c_r, gc_s, gc_r, gy_s, gy_r, ag_s, ag_r, ac_s, ac_r, ha_s, ha_r,
):
    n = NX * NZ
    dp, me, y, c, x, z, partner = place()
    rows, width = table_v.shape
    slots = fetched.shape[1]
    half = hot.shape[3]
    hot_dev = 2 * half
    hot_cols = n * hot_dev
    per_y = hz.shape[1]
    batch, vocab = inc.shape
    parts = hc_s.shape[0]
    subs, sub = gl.shape[1], gl.shape[3]

    def dp_of(yy):
        return yy * 2 + c

    def over(lo, hi, body, unroll=1):
        def run(k, _):
            body(k)
            return 0

        lax.fori_loop(lo, hi, run, 0, unroll=unroll)

    def other(k):
        return ring(me + 1 + k, n)

    def eye(a, b, shift=0):
        return lax.broadcasted_iota(i32, (a, b), 0) + shift == lax.broadcasted_iota(i32, (a, b), 1)

    def to_column(mask, row):
        return jnp.sum(jnp.where(mask, row, 0.0), axis=1, keepdims=True)

    barrier = pltpu.get_barrier_semaphore()
    over(0, n - 1, lambda k: pl.semaphore_signal(
        barrier, inc=1, device_id=(dp, peer(k, x, z)), device_id_type=MESH))
    over(1, 2 * NY, lambda k: pl.semaphore_signal(
        barrier, inc=1, device_id=(ring(dp + k, 2 * NY), me), device_id_type=MESH))

    small = (
        (ids_hbm, ids_ref), (hot_ids_hbm, hot_ids_ref), (bag_hbm, bag_ref), (w_out_hbm, w_out_ref),
        (count_hbm, count_ref), (sum_hbm, sum_ref), (labels_hbm, labels_ref),
    )
    loads = [pltpu.make_async_copy(a, b, in_s.at[i + 2]) for i, (a, b) in enumerate(small)]
    load_table = pltpu.make_async_copy(table_hbm, table_v, in_s.at[0])
    load_w = pltpu.make_async_copy(w_hbm, w_v, in_s.at[1])
    for load in loads[:2]:
        load.start()
    load_table.start()
    for load in loads[2:]:
        load.start()
    load_w.start()
    for load in loads:
        load.wait()

    ids3[...] = jnp.full_like(ids3, -1)
    for t in range(n):
        ids3[t, :, pl.ds(0, slots)] = ids_ref[pl.ds(t, 1), :]
    hot_pad[...] = jnp.full_like(hot_pad, -1)
    hot_pad[:, pl.ds(0, hot_dev)] = hot_ids_ref[...]
    for k in range(w_out_ref.shape[0]):
        w_row[:, pl.ds(k * 128, 128)] = w_out_ref[pl.ds(k, 1), :].astype(f32)
    lane = lax.broadcasted_iota(i32, (1, slots), 1)
    for t in range(n):
        live[:, pl.ds(t * slots, slots)] = (lane < count_ref[:, t : t + 1]).astype(f32)
    bag = bag_ref.shape[0]
    bag_rows[...] = bag_ref[...].T
    for s in range(8):
        bag2[:, pl.ds(s * bag, bag)] = bag_rows[pl.ds(s, batch // 8, stride=8), :]

    entries = 8 * bag
    tiles = vocab // 128
    own = lax.broadcasted_iota(i32, (8, entries), 1) // bag == lax.broadcasted_iota(i32, (8, entries), 0)
    tile_ids = lax.broadcasted_iota(i32, (tiles, 8, entries), 0)
    lane_ids = lax.broadcasted_iota(i32, (128, entries), 0)

    def build(i):
        outs = []
        for h in range(2):
            v = bag2[pl.ds(2 * i + h, 1), :]
            key = jnp.where(own, v >> 7, -1)
            left = (key[None] == tile_ids).astype(f32).reshape(tiles * 8, entries).astype(bf16)
            right = (lane_ids == (v & 127)).astype(f32).astype(bf16)
            outs.append(
                lax.dot_general(left, right, (((1,), (1,)), ((), ())), preferred_element_type=f32)
            )
        at = pl.ds(pl.multiple_of(16 * i, 16), 16)
        for k in range(tiles):
            t = jnp.concatenate([outs[0][8 * k : 8 * k + 8], outs[1][8 * k : 8 * k + 8]], axis=0)
            if k * 128 >= hot_cols:
                t = t * live[:, pl.ds(k * 128 - hot_cols, 128)]
            inc[at, pl.ds(k * 128, 128)] = t.astype(bf16)

    load_table.wait()
    tb[...] = table_v[...].astype(bf16)
    hot_col = to_column(eye(half, 128, c * half), hot_pad[...].astype(f32))
    hot_sel = (hot_col == lax.broadcasted_iota(i32, (half, rows), 1).astype(f32)).astype(f32).astype(bf16)
    hot[x, z, c] = jnp.dot(hot_sel, tb[...], preferred_element_type=f32).astype(bf16)
    asked[me] = ids3[me]
    over(0, pre, build)
    pl.semaphore_wait(barrier, n - 1 + 2 * NY - 1)

    def send_ids(k):
        p = peer(k, x, z)
        remote(ids3.at[p], asked.at[me], ids_s.at[p], ids_r.at[me], dp, p).start()

    over(0, n - 1, send_ids)

    def hot_to_x(zs, xo):
        blk_ = hot.at[x, zs, c]
        remote(blk_, blk_, xb_s.at[xo, zs], xb_r.at[x, zs], dp, (ring(x + xo, NX)) * NZ + z).start()

    def hot_to_z(zo):
        blk_ = hot.at[x, z, c]
        remote(blk_, blk_, za_s.at[zo], za_r.at[z], dp, x * NZ + ring(z + zo, NZ)).start()

    over(1, NZ, hot_to_z)
    for xo in range(1, NX):
        hot_to_x(z, xo)
    over(pre, mid, build)

    def forward_x(zo):
        zs = ring(z + zo, NZ)
        blk_ = hot.at[x, zs, c]
        remote(blk_, blk_, za_s.at[zo], za_r.at[zs], dp, me).wait_recv()
        for xo in range(1, NX):
            hot_to_x(zs, xo)

    request = eye(slots, 128)
    chunk = served.shape[1] // slots

    def serve(ch):
        for j in range(chunk):
            k = ch * chunk + j
            p = peer(ring(2 * n - 2 - k, n), x, z)

            def arrived():
                remote(ids3.at[p], asked.at[p], ids_s.at[p], ids_r.at[p], dp, p).wait_recv()

            if j == chunk - 1:
                pl.when(k < n - 1)(arrived)
            else:
                arrived()
            col = to_column(request, asked[p].astype(f32))
            hit = col == lax.broadcasted_iota(i32, (slots, rows), 1).astype(f32)
            oh[pl.ds(j * slots, slots), :] = hit.astype(f32).astype(bf16)
        served[ch] = jnp.dot(oh[...], tb[...], preferred_element_type=f32).astype(bf16)
        for j in range(chunk):
            k = ch * chunk + j
            p = peer(ring(2 * n - 2 - k, n), x, z)
            block = served.at[ch, pl.ds(j * slots, slots)]

            def send():
                remote(block, fetched.at[me], f_s.at[p], f_r.at[me], dp, p).start()

            def keep():
                fetched[me] = served[ch, pl.ds(j * slots, slots)]

            if j == chunk - 1:
                pl.when(k < n - 1)(send)
                pl.when(k == n - 1)(keep)
            else:
                send()

    chunks = n // chunk
    over(0, chunks // 2, serve)
    over(1, NZ, forward_x)
    line = hot.at[x, :, c]
    remote(line, line, cc_s.at[x], cc_r.at[x], partner, me).start()
    over(chunks // 2, chunks, serve)
    over(mid, batch // 16, build)

    def line_to_partner(xo):
        xs = ring(x + xo, NX)

        def landed(zs):
            blk_ = hot.at[xs, zs, c]
            remote(blk_, blk_, xb_s.at[xo, zs], xb_r.at[xs, zs], dp, me).wait_recv()

        over(0, NZ, landed)
        line = hot.at[xs, :, c]
        remote(line, line, cc_s.at[xs], cc_r.at[xs], partner, me).start()

    over(1, NX, line_to_partner)

    for t in range(n):
        flat[:, pl.ds(t * slots, slots)] = asked[t][:, :slots]
    for b in range(rows // 128):
        sum_col[pl.ds(b * 128, 128), :] = to_column(eye(128, 128), sum_ref[pl.ds(b, 1), :])

    def finish_x(xs):
        line = hot.at[xs, :, 1 - c]
        remote(line, line, cc_s.at[xs], cc_r.at[xs], partner, me).wait_recv()

    over(0, NX, finish_x)
    acc[...] = jnp.dot(
        inc[:, pl.ds(0, hot_cols)], hot[...].reshape(hot_cols, width), preferred_element_type=f32
    )

    lab = jnp.concatenate(
        [to_column(eye(128, 128), labels_ref[:, pl.ds(b * 128, 128)]) for b in range(batch // 128)], axis=0
    )

    def fetched_wait(k):
        p = other(k)
        remote(fetched.at[p], fetched.at[p], f_s.at[p], f_r.at[p], dp, p).wait_recv()

    over(0, n - 1, fetched_wait)
    pooled = (
        acc[...]
        + jnp.dot(
            inc[:, pl.ds(hot_cols, vocab - hot_cols)],
            fetched[...].reshape(n * slots, width),
            preferred_element_type=f32,
        )
    ).astype(bf16)

    load_w.wait()
    acc[...] = jnp.zeros_like(acc)
    hidden_units = w_v.shape[1]
    step = acc.shape[1]

    def forward(j):
        at = pl.ds(pl.multiple_of(j * step, step), step)
        pre_act = jnp.dot(pooled, w_v[:, at], preferred_element_type=f32)
        w = w_row[:, at]
        acc[...] += jnp.maximum(pre_act, 0.0).astype(bf16).astype(f32) * w
        wm[:, at] = jnp.where(pre_act > 0, w, 0.0).astype(bf16)

    over(0, hidden_units // step, forward, unroll=4)
    logit = jnp.sum(acc[...], axis=1, keepdims=True)
    dlogit = jax.nn.sigmoid(logit) - lab
    dpool[...] = jnp.zeros_like(dpool)
    deep = min(1024, hidden_units)

    def backward(j):
        at = pl.ds(pl.multiple_of(j * deep, deep), deep)
        dhidden = (dlogit * wm[:, at].astype(f32)).astype(bf16)
        dpool[...] += lax.dot_general(
            dhidden, w_v[:, at], (((1,), (1,)), ((), ())), preferred_element_type=f32
        )

    over(0, hidden_units // deep, backward, unroll=2 if hidden_units > deep else 1)
    dpooled = dpool[...].astype(bf16)

    def slot_grad(at, size):
        return lax.dot_general(
            inc[:, pl.ds(at, size)], dpooled, (((0,), (0,)), ((), ())), preferred_element_type=f32
        )

    def core_copy(q):
        at = pl.ds(q * (n // parts), n // parts)
        return remote(hot_g.at[1 - c, at], hcore.at[at], hc_s.at[q], hc_r.at[q], partner, me)

    cold_step = min(256, n * slots)
    for k in range(n * slots // cold_step):
        g = slot_grad(hot_cols + k * cold_step, cold_step)
        for i in range(cold_step // slots):
            t = k * (cold_step // slots) + i
            cold_g[t] = g[i * slots : (i + 1) * slots].astype(bf16)

    def cold_send(k):
        p = peer(k, x, z)
        to = ret.at[pl.ds(pl.multiple_of(me * slots, slots), slots)]
        remote(cold_g.at[p], to, c_s.at[p], c_r.at[me], dp, p).start()

    over(0, n - 1, cold_send)
    owners = 256 // hot_dev
    for k in range(hot_cols // 256):
        g = slot_grad(k * 256, 256).reshape(owners, NY, per_y, width).astype(bf16)
        for h in range(2):
            hot_g[h, pl.ds(k * owners, owners)] = g[..., h * 128 : (h + 1) * 128]
        done = (k + 1) * parts
        if done % (hot_cols // 256) == 0:
            core_copy(done // (hot_cols // 256) - 1).start()

    def y_copy(src, yt, q):
        at = pl.ds(q * (n // parts), n // parts)
        return remote(hsum.at[yt, at], hy.at[src, at], hy_s.at[yt, q], hy_r.at[src, q], dp_of(yt), me)

    for r in range(0, rows, 128):
        ids = lax.broadcasted_iota(i32, (128, n * slots), 0) + r
        oht[pl.ds(r, 128), :] = (ids == flat[...]).astype(f32).astype(bf16)
    for q in range(parts):
        core_copy(q).wait_recv()
        at = pl.ds(q * (n // parts), n // parts)

        def y_send(k):
            yt = y_peer(k, y)
            hsum[yt, at] = (hot_g[c, at, yt].astype(f32) + hcore[at, yt].astype(f32)).astype(bf16)

            @pl.when(k < NY - 1)
            def _():
                y_copy(y, yt, q).start()

        over(0, NY, y_send)
    ret[pl.ds(pl.multiple_of(me * slots, slots), slots), :] = cold_g[me]
    hsel[...] = (lax.broadcasted_iota(i32, (rows, 128), 0) == hot_pad[...]).astype(f32).astype(bf16)
    hfin[...] = jnp.zeros_like(hfin)

    def finish_fetch(k):
        p = other(k)
        remote(ids3.at[p], asked.at[me], ids_s.at[p], ids_r.at[me], dp, p).wait_send()
        remote(served.at[0, pl.ds(0, slots)], fetched.at[me], f_s.at[p], f_r.at[me], dp, p).wait_send()

    over(0, n - 1, finish_fetch)

    def finish_hot(zo):
        blk_ = hot.at[x, z, c]

        @pl.when(zo > 0)
        def _():
            remote(blk_, blk_, za_s.at[zo], za_r.at[z], dp, me).wait_send()

        for xo in range(1, NX):
            remote(blk_, blk_, xb_s.at[xo, zo], xb_r.at[x, zo], dp, me).wait_send()

    over(0, NZ, finish_hot)

    def finish_line(xs):
        line = hot.at[xs, :, c]
        remote(line, line, cc_s.at[xs], cc_r.at[xs], partner, me).wait_send()

    over(0, NX, finish_line)
    def cold_wait(k):
        p = other(k)
        to = ret.at[pl.ds(pl.multiple_of(p * slots, slots), slots)]
        remote(cold_g.at[p], to, c_s.at[p], c_r.at[p], dp, p).wait_recv()

    over(0, n - 1, cold_wait)

    pieces = 2
    per = subs // pieces
    piece_rows = rows // 2 // pieces

    def piece_grad(cc, i):
        at = pl.ds(pl.multiple_of(cc * (rows // 2) + i * piece_rows, piece_rows), piece_rows)
        g = jnp.dot(oht[at, :], ret[...], preferred_element_type=f32)
        gl[cc, pl.ds(i * per, per)] = g.astype(bf16).reshape(per, NY, sub, width)

    def g_core(b):
        return remote(gl.at[1 - c, b], gcore.at[b], gc_s.at[b], gc_r.at[b], partner, me)

    def g_y(b, src, yt):
        return remote(gsum.at[b, yt], gy.at[b, src], gy_s.at[b, yt], gy_r.at[b, src], dp_of(yt), me)

    for i in range(pieces):
        piece_grad(1 - c, i)
        over(i * per, (i + 1) * per, lambda b: g_core(b).start())

    def g_send(b):
        g_core(b).wait_recv()
        gsum[b] = (gl[c, b].astype(f32) + gcore[b].astype(f32)).astype(bf16)
        over(0, NY - 1, lambda k: g_y(b, y, y_peer(k, y)).start())

    for i in range(pieces):
        piece_grad(c, i)
        over(i * per, (i + 1) * per, g_send)

    def y_wait(k):
        ys = ring(y + k, NY)
        for q in range(parts):
            y_copy(ys, ys, q).wait_recv()

    over(1, NY, y_wait)
    hy[y] = hsum[y]
    tot = hy[0].astype(f32)
    for k in range(1, NY):
        tot = tot + hy[k].astype(f32)
    hz[...] = tot.astype(bf16)

    def t_send(k):
        p = peer(k, x, z)
        remote(hz.at[p], ht.at[me], ht_s.at[p], ht_r.at[me], dp, p).start()

    over(0, n - 1, t_send)
    ht[me] = hz[me]

    def to_y(b, src, yt):
        part = total.at[c, b, src]
        return remote(part, part, ag_s.at[b, yt], ag_r.at[b, src], dp_of(yt), me)

    def to_core(cc, b, yt):
        part = total.at[cc, b, yt]
        return remote(part, part, ac_s.at[b, yt], ac_r.at[b, yt], partner, me)

    def dp_sum(b):
        over(1, NY, lambda k: g_y(b, ring(y + k, NY), ring(y + k, NY)).wait_recv())
        gy[b, y] = gsum[b, y]
        tot = gy[b, 0].astype(f32)
        for k in range(1, NY):
            tot = tot + gy[b, k].astype(f32)
        total[c, b, y] = tot.astype(bf16)
        over(0, NY - 1, lambda k: to_y(b, y, y_peer(k, y)).start())
        to_core(c, b, y).start()

    over(0, subs, dp_sum)

    def t_wait(k):
        p = other(k)
        remote(hz.at[p], ht.at[p], ht_s.at[p], ht_r.at[p], dp, p).wait_recv()

    over(0, n - 1, t_wait)
    hotf[c, pl.ds(pl.multiple_of(y * per_y, 8), per_y), :] = jnp.sum(ht[...].astype(f32), axis=0)

    def h_copy(src, to):
        b = hotf.at[lax.rem(src, 2), pl.ds(pl.multiple_of(lax.div(src, 2) * per_y, 8), per_y)]
        return remote(b, b, ha_s.at[to], ha_r.at[src], to, me)

    over(1, 2 * NY, lambda k: h_copy(dp, ring(dp + k, 2 * NY)).start())

    def h_wait(k):
        src = ring(dp + k, 2 * NY)
        h_copy(src, src).wait_recv()

    def update(cc, b):
        tall = NY * sub
        at = pl.ds(pl.multiple_of((cc * subs + b) * tall, tall), tall)
        g = total[cc, b].astype(f32).reshape(tall, width) + gacc[at, :]
        new_sum = sum_col[at, :] + jnp.sum(g * g, axis=1, keepdims=True) * (1.0 / width)
        sum_col[at, :] = new_sum
        if tall == 128:
            sum_out[pl.ds(cc * subs + b, 1), :] = jnp.sum(
                jnp.where(eye(128, 128), new_sum, 0.0), axis=0, keepdims=True
            )
        table_out[at, :] = table_v[at, :] - g * (learning_rate / jnp.sqrt(new_sum))

    def gather(b):
        def landed(k):
            ys = ring(y + k, NY)
            to_y(b, ys, ys).wait_recv()
            to_core(c, b, ys).start()

        over(1, NY, landed)

    def finish_table(k):
        p = other(k)
        to = ret.at[pl.ds(pl.multiple_of(me * slots, slots), slots)]
        remote(cold_g.at[p], to, c_s.at[p], c_r.at[me], dp, p).wait_send()
        remote(hz.at[p], ht.at[me], ht_s.at[p], ht_r.at[me], dp, p).wait_send()

    def finish_sums(k):
        yt = ring(y + k, NY)
        for q in range(parts):
            y_copy(y, yt, q).wait_send()
        over(0, subs, lambda b: g_y(b, y, yt).wait_send())

    over(0, subs // 2, gather)
    over(0, n - 1, finish_table)
    over(1, NY, finish_sums)
    for q in range(parts):
        core_copy(q).wait_send()
    over(0, subs, lambda b: g_core(b).wait_send())
    over(1, 2 * NY, h_wait)
    for h in range(2):
        hfin[pl.ds(0, hot_dev), pl.ds(h * 128, 128)] = hotf[h]
    gacc[...] = jnp.dot(hsel[...], hfin[...].astype(bf16), preferred_element_type=f32)
    over(0, subs // 2, lambda b: update(c, b))

    def gather_update(b):
        gather(b)
        update(c, b)

    over(subs // 2, subs, gather_update)

    def gather_core(b):
        over(0, NY, lambda k: to_core(1 - c, b, k).wait_recv())
        update(1 - c, b)

    over(0, subs - 1, gather_core)

    def finish_y(k):
        yt = ring(y + k, NY)
        over(0, subs, lambda b: to_y(b, y, yt).wait_send())

    over(1, NY, finish_y)
    over(1, 2 * NY, lambda k: h_copy(dp, ring(dp + k, 2 * NY)).wait_send())
    over(0, subs * NY, lambda k: to_core(c, lax.div(k, NY), ring(k, NY)).wait_send())
    gather_core(subs - 1)
    if NY * sub != 128:
        for b in range(rows // 128):
            sum_out[pl.ds(b, 1), :] = jnp.sum(
                jnp.where(eye(128, 128), sum_col[pl.ds(b * 128, 128), :], 0.0), axis=0, keepdims=True
            )


def emit_kernel(table_ref, sum_ref, table_out, sum_out, sems):
    copies = [
        pltpu.make_async_copy(table_ref, table_out, sems.at[0]),
        pltpu.make_async_copy(sum_ref, sum_out, sems.at[1]),
    ]
    for copy in copies:
        copy.start()
    for copy in copies:
        copy.wait()


def per_device(bag_slots, labels, cold_ids, cold_count, table, adagrad_sum, hot_ids, w_in, w_out):
    n = NX * NZ
    batch, bag = bag_slots.shape
    rows, width = table.shape
    slots = cold_ids.shape[2]
    hot_dev = hot_ids.shape[0]
    hot_cols = n * hot_dev
    vocab = n * (hot_dev + slots)
    hidden = w_in.shape[1]
    chunk = min(8, n)
    per_y = hot_dev // NY
    parts = 2 if hot_cols % 512 == 0 else 1
    sub = 16
    subs = rows // (2 * NY * sub)
    groups = batch // 16
    dma = pltpu.SemaphoreType.DMA
    vmem = pl.BlockSpec(memory_space=pltpu.VMEM)
    hbm = pl.BlockSpec(memory_space=pltpu.HBM)
    new_table, new_sum = pl.pallas_call(
        functools.partial(step_kernel, groups // 4, groups // 2),
        name="step",
        out_shape=(
            jax.ShapeDtypeStruct((rows, width), f32),
            jax.ShapeDtypeStruct((rows // 128, 128), f32),
        ),
        in_specs=[hbm] * 9,
        out_specs=(vmem, vmem),
        scratch_shapes=[
            pltpu.VMEM((bag, batch), i32),
            pltpu.VMEM((1, batch), f32),
            pltpu.VMEM((n, slots), i32),
            pltpu.VMEM((1, n), i32),
            pltpu.VMEM((rows // 128, 128), f32),
            pltpu.VMEM((1, hot_dev), i32),
            pltpu.VMEM((hidden // 128, 128), bf16),
            pltpu.VMEM((rows, width), f32),
            pltpu.VMEM(w_in.shape, bf16),
            pltpu.VMEM((rows, width), bf16),
            pltpu.VMEM((n, 1, 128), i32),
            pltpu.VMEM((n, 1, 128), i32),
            pltpu.VMEM((1, n * slots), i32),
            pltpu.VMEM((1, 128), i32),
            pltpu.VMEM((batch, bag), i32),
            pltpu.VMEM((batch // 8, 8 * bag), i32),
            pltpu.VMEM((rows, 1), f32),
            pltpu.VMEM((NX, NZ, 2, hot_dev // 2, width), bf16),
            pltpu.VMEM((n, slots, width), bf16),
            pltpu.VMEM((chunk * slots, rows), bf16),
            pltpu.VMEM((n // chunk, chunk * slots, width), bf16),
            pltpu.VMEM((batch, vocab), bf16),
            pltpu.VMEM((batch, hidden), bf16),
            pltpu.VMEM((batch, 256), f32),
            pltpu.VMEM((batch, width), f32),
            pltpu.VMEM((2, n, NY, per_y, 128), bf16),
            pltpu.VMEM((n, slots, width), bf16),
            pltpu.VMEM((n, NY, per_y, 128), bf16),
            pltpu.VMEM((NY, n, per_y, 128), bf16),
            pltpu.VMEM((NY, n, per_y, 128), bf16),
            pltpu.VMEM((n, per_y, 128), bf16),
            pltpu.VMEM((n, per_y, 128), bf16),
            pltpu.VMEM((n * slots, width), bf16),
            pltpu.VMEM((rows, n * slots), bf16),
            pltpu.VMEM((rows, width), f32),
            pltpu.VMEM((128, width), f32),
            pltpu.VMEM((rows, 128), bf16),
            pltpu.VMEM((2, hot_dev, 128), f32),
            pltpu.VMEM((1, hidden), f32),
            pltpu.VMEM((1, n * slots), f32),
            pltpu.VMEM((2, subs, NY, sub, width), bf16),
            pltpu.VMEM((subs, NY, sub, width), bf16),
            pltpu.VMEM((subs, NY, sub, width), bf16),
            pltpu.VMEM((subs, NY, sub, width), bf16),
            pltpu.VMEM((2, subs, NY, sub, width), bf16),
            dma((9,)),
            dma((n,)), dma((n,)),
            dma((NZ,)), dma((NZ,)),
            dma((NX, NZ)), dma((NX, NZ)),
            dma((NX,)), dma((NX,)),
            dma((n,)), dma((n,)),
            dma((parts,)), dma((parts,)),
            dma((NY, parts)), dma((NY, parts)),
            dma((n,)), dma((n,)),
            dma((n,)), dma((n,)),
            dma((subs,)), dma((subs,)),
            dma((subs, NY)), dma((subs, NY)),
            dma((subs, NY)), dma((subs, NY)),
            dma((subs, NY)), dma((subs, NY)),
            dma((2 * NY,)), dma((2 * NY,)),
        ],
        compiler_params=pltpu.CompilerParams(
            collective_id=0, has_side_effects=True, vmem_limit_bytes=44 << 20
        ),
    )(*[pltpu.with_memory_space_constraint(v, pltpu.HBM) for v in (
        table,
        w_in,
        bag_slots.T,
        labels.reshape(1, batch),
        cold_ids[0],
        cold_count,
        adagrad_sum.reshape(rows // 128, 128),
        hot_ids.reshape(1, hot_dev),
        w_out.reshape(hidden // 128, 128),
    )])
    out_table, out_sum = pl.pallas_call(
        emit_kernel,
        name="emit",
        out_shape=(
            jax.ShapeDtypeStruct((rows, width), f32),
            jax.ShapeDtypeStruct((rows // 128, 128), f32),
        ),
        in_specs=[vmem, vmem],
        out_specs=(hbm, hbm),
        scratch_shapes=[dma((2,))],
        compiler_params=pltpu.CompilerParams(vmem_limit_bytes=4 << 20),
    )(new_table, new_sum)
    return out_table, out_sum.reshape(rows)


def solution(mesh):
    placed = (
        P(("dp", "table"), None),
        P(("dp", "table")),
        P(("dp", "table"), None, None),
        P(("dp", "table"), None),
        P("table", None),
        P("table"),
        P("table"),
        P(),
        P(),
    )
    return jax.shard_map(
        per_device,
        mesh=mesh,
        in_specs=placed,
        out_specs=(P("table", None), P("table")),
        check_vma=False,
    )
```
